256 devices in a mesh: seq: 32 (over y_hi, z, core), head: 8 (over x, y_lo).
Axes of the slice: x: 4, y: 4 (y_hi: 2, y_lo: 2; y = y_hi * 2 + y_lo), z: 8, core: 2. Of those that a mesh axis runs over, the one named last changes fastest.
Arguments:
- queries: bfloat16 [49152, 4096], P('seq', 'head'), may hold values from -6 to 6, as said below
- keys: bfloat16 [49152, 2048], P('seq', 'head'), may hold values from -6 to 6
- values: bfloat16 [49152, 2048], P('seq', 'head'), may hold values from -6 to 6
- q_gain: float32 [128], replicated, may hold values from -0.5 to 5
- k_gain: float32 [128], replicated, may hold values from -0.5 to 5
- positions: int32 [49152], P('seq'), may hold values from 2048 to 52222, as said below
- prefix_cache: bfloat16 [32, 2048, 4096], P('seq', 'head'), may hold values from -6 to 6
- owner: int32 [1], replicated, may hold values from 0 to 31
Outputs:
- attended: bfloat16 [49152, 4096], P('seq', 'head')
The draws below stay inside these ranges and needn't reach their ends.
Inputs may be any that keep to these rules, and one draw needn't show every extreme that they name: queries and keys are of order one. positions[i] = positions[0] + i, and positions[0] is 2048 or more and under 2048 + 1024.
All inputs are finite; a program needn't handle non-finite values.
Results may differ from the reference program's by a relative error of at most 0.02.
Values may be sent and summed in bfloat16 or wider, within the bound.
No kernel may reach another device: no remote copies, remote signals or barrier semaphores. Data moves between devices by JAX's collectives and lax.ppermute only.
A program may use at most 128 MiB of HBM per device.

```python
import jax
import jax.numpy as jnp
from jax import lax

HD = 128
QH = 32
KVH = 16
WINDOW = 1024
QSCALAR = 168
PREFIX = 2048
BLOCK = 512
TOKENS = 49152
N_SEQ = 32


def paired_draw(key):
    key_q = jax.random.fold_in(key, 11)
    key_k = jax.random.fold_in(key, 12)
    query_part = jnp.clip(jax.random.normal(key_q, (TOKENS, QH * HD), jnp.float32), -6.0, 6.0)
    key_part = jnp.clip(jax.random.normal(key_k, (TOKENS, KVH * HD), jnp.float32), -6.0, 6.0)
    return (query_part, key_part)


def draw_queries(key, part):
    return paired_draw(key)[0].astype(jnp.bfloat16)


def draw_keys(key, part):
    return paired_draw(key)[1].astype(jnp.bfloat16)


def gain_draw(key):
    return jax.random.uniform(key, (HD,), jnp.float32, -0.5, 1.5)


def draw_q_gain(key, part):
    return gain_draw(jax.random.fold_in(key, 21))


def draw_k_gain(key, part):
    return gain_draw(jax.random.fold_in(key, 22))


def draw_positions(key, part):
    start = jax.random.randint(jax.random.fold_in(key, 31), (), PREFIX, PREFIX + 1024, jnp.int32)
    return (start + jnp.arange(TOKENS, dtype=jnp.int32)).astype(jnp.int32)


def block_scale(key, extent, shards, smallest, largest):
    def one(axis_at, shards_of):
        draws = jax.random.uniform(jax.random.fold_in(jax.random.fold_in(key, 6), axis_at), (shards_of,), jnp.float32, smallest / len(shards), largest / len(shards))
        return jnp.repeat(jnp.exp(draws), extent[axis_at] // shards_of).reshape((-1,) + (1,) * (len(extent) - axis_at - 1))

    level = one(*shards[0])
    for cut in shards[1:]:
        level = level * one(*cut)
    return level


def centred(key, dims, deviation, most, shards=(), kind=jnp.bfloat16):
    values = jax.random.normal(key, dims, jnp.float32) * deviation
    if len(shards) > 0:
        values = block_scale(key, dims, shards, -0.22, 0.18) * values
    return jnp.clip(values, min=-most, max=most).astype(kind)


def setup_inputs(seed: int = 0) -> dict:
    streams_of = jax.random.split(jax.random.key(seed), 9)
    queries = draw_queries(jax.random.fold_in(streams_of[8], 71), 0)
    keys = draw_keys(jax.random.fold_in(streams_of[8], 71), 0)
    values = centred(streams_of[2], (TOKENS, KVH * HD), 1.0, 6.0, ((0, 32), (1, 8)))
    q_gain = draw_q_gain(jax.random.fold_in(streams_of[8], 71), 0)
    k_gain = draw_k_gain(jax.random.fold_in(streams_of[8], 71), 0)
    positions = draw_positions(jax.random.fold_in(streams_of[8], 71), 0)
    prefix_cache = centred(streams_of[6], (N_SEQ, PREFIX, 2 * KVH * HD), 1.0, 6.0, ((0, 32), (1, 8)))
    owner = jax.random.randint(streams_of[7], (1,), 0, N_SEQ).astype(jnp.int32)
    return dict(queries=queries, keys=keys, values=values, q_gain=q_gain, k_gain=k_gain, positions=positions, prefix_cache=prefix_cache, owner=owner)


def norm_rope(rows_in, gain, pos, factor):
    mean_sq = lax.optimization_barrier(jnp.mean(rows_in * rows_in, axis=-1, keepdims=True))
    normed = rows_in / jnp.sqrt(mean_sq + 1e-06) * (1.0 + gain)
    half = rows_in.shape[-1] // 2
    freq = 10000.0 ** (-(jnp.arange(half).astype(jnp.float32) * 2.0) / rows_in.shape[-1])
    angle = pos.astype(jnp.float32)[:, None] * freq[None, :]
    cosine = jnp.cos(angle)[:, None, :]
    sine = jnp.sin(angle)[:, None, :]
    first = normed[..., :half]
    second = normed[..., half:]
    return jnp.concatenate([first * cosine - second * sine, second * cosine + first * sine], axis=-1) * factor

def reference(queries, keys, values, q_gain, k_gain, positions, prefix_cache, owner):
    total_rows = queries.shape[0]
    group = QH // KVH
    query = norm_rope(queries.astype(jnp.float32).reshape(total_rows, QH, HD), q_gain, positions, QSCALAR ** (-0.5)).astype(jnp.bfloat16)
    key = norm_rope(keys.astype(jnp.float32).reshape(total_rows, KVH, HD), k_gain, positions, 1.0).astype(jnp.bfloat16)
    value = values.reshape(total_rows, KVH, HD)
    slot = lax.dynamic_index_in_dim(prefix_cache, owner[0].astype(jnp.int32), 0, keepdims=False)
    slot = slot.reshape(PREFIX, KVH, 2, HD)
    prefix_key = slot[:, :, 0, :].astype(jnp.float32)
    prefix_value = slot[:, :, 1, :].astype(jnp.float32)
    key_pad = jnp.concatenate([jnp.zeros((WINDOW, KVH, HD), jnp.bfloat16), key], axis=0)
    value_pad = jnp.concatenate([jnp.zeros((WINDOW, KVH, HD), jnp.bfloat16), value], axis=0)

    def one_block(index):
        start = (index * BLOCK).astype(jnp.int32)
        query_block = lax.dynamic_slice_in_dim(query, start, BLOCK, 0).reshape(BLOCK, KVH, group, HD).astype(jnp.float32)
        key_block = lax.dynamic_slice_in_dim(key_pad, start, WINDOW + BLOCK, 0).astype(jnp.float32)
        value_block = lax.dynamic_slice_in_dim(value_pad, start, WINDOW + BLOCK, 0).astype(jnp.float32)
        band = jnp.einsum('ikgd,jkd->kgij', query_block, key_block)
        row_pos = start + jnp.arange(BLOCK, dtype=jnp.int32)
        col_pos = start + jnp.arange(WINDOW + BLOCK, dtype=jnp.int32) - WINDOW
        valid = (col_pos[None, :] >= 0) & (col_pos[None, :] <= row_pos[:, None]) & (col_pos[None, :] > row_pos[:, None] - WINDOW)
        band = jnp.where(valid[None, None], band, -jnp.inf)
        pre = jnp.einsum('ikgd,tkd->kgit', query_block, prefix_key)
        top = jnp.maximum(lax.optimization_barrier(jnp.max(band, axis=-1)), lax.optimization_barrier(jnp.max(pre, axis=-1)))
        exp_band = jnp.exp(band - top[..., None])
        exp_pre = jnp.exp(pre - top[..., None])
        total = lax.optimization_barrier(jnp.sum(exp_band, axis=-1)) + lax.optimization_barrier(jnp.sum(exp_pre, axis=-1))
        weight_band = exp_band.astype(jnp.bfloat16).astype(jnp.float32)
        weight_pre = exp_pre.astype(jnp.bfloat16).astype(jnp.float32)
        summed = jnp.einsum('kgij,jkd->kgid', weight_band, value_block) + jnp.einsum('kgit,tkd->kgid', weight_pre, prefix_value)
        result = summed / total[..., None]
        return jnp.transpose(result, (2, 0, 1, 3)).reshape(BLOCK, QH * HD).astype(jnp.bfloat16)
    blocks = lax.map(one_block, jnp.arange(total_rows // BLOCK, dtype=jnp.int32))
    return blocks.reshape(total_rows, QH * HD)
```

```python
import functools

import jax
import jax.numpy as jnp
from jax import lax
from jax.experimental import pallas as pl
from jax.experimental.pallas import tpu as pltpu
from jax.sharding import PartitionSpec as P

HD = 128
WINDOW = 1024
QSCALAR = 168
YH, NZ, NC = 2, 8, 2
TILE = 256
NEG = -1e30
VMEM_LIMIT = 56 * 1024 * 1024


def where_is(i):
    return i // (NZ * NC), (i // NC) % NZ, i % NC


def hop(array, move):
    route = []
    for i in range(YH * NZ * NC):
        y, z, c = move(*where_is(i))
        route.append((i, (y * NZ + z) * NC + c))
    return lax.ppermute(array, "seq", route)


def other_core(array):
    return hop(array, lambda y, z, c: (y, z, 1 - c))


def other_half(array):
    return hop(array, lambda y, z, c: (1 - y, z, c))


def round_z(array, r):
    return hop(array, lambda y, z, c: (y, (z + r) % NZ, c))


ROUNDS = (4, 3, 5, 2, 6, 1, 7)


def pick(array, at):
    return lax.dynamic_index_in_dim(array, at, 0, keepdims=False)


def scatter_from(slab, root):
    me = lax.axis_index("seq")
    y, z, c = where_is(me)
    root_y, root_z, root_c = where_is(root)
    rows, columns = slab.shape
    part = slab.reshape(NC, rows // NC, columns)
    came = other_core(pick(part, 1 - c))
    part = jnp.where(root_c == c, pick(part, c), came)
    part = part.reshape(YH, -1, columns)
    came = other_half(pick(part, 1 - y))
    part = jnp.where(root_y == y, pick(part, y), came)
    part = part.reshape(NZ, -1, columns)
    kept = pick(part, z)
    for r in ROUNDS:
        came = round_z(pick(part, (z + r) % NZ), r)
        kept = jnp.where(root_z == (z - r) % NZ, came, kept)
    return kept


def normed(rows, gain, cosine, sine):
    mean_sq = jnp.mean(rows * rows, axis=-1, keepdims=True)
    rows = rows * lax.rsqrt(mean_sq + 1e-06) * gain
    return rows * cosine + pltpu.roll(rows, HD // 2, 1) * sine


def dot_t(a, b):
    return lax.dot_general(a, b, (((1,), (1,)), ((), ())), preferred_element_type=jnp.float32)


def pack_state(parts):
    lane = lax.broadcasted_iota(jnp.int32, (TILE, HD), 1)
    packed = jnp.zeros((TILE, HD), jnp.float32)
    for at, part in enumerate(parts):
        packed = jnp.where(lane == at, part, packed)
    return packed


def band_kernel(
    first_ref, q_ref, kh_ref, k_ref, vh_ref, v_ref, qg_ref, kg_ref, cos_ref, sin_ref,
    qn_ref, acc_ref, ml_ref, kn_ref, va_ref,
):
    local = q_ref.shape[0]
    local_kv = k_ref.shape[1] // HD
    group = q_ref.shape[1] // HD // local_kv
    ones = jnp.ones((WINDOW, HD), jnp.bfloat16)
    for c in range(local_kv):
        columns = slice(c * HD, (c + 1) * HD)
        va_ref[:WINDOW, 2 * c * HD : (2 * c + 1) * HD] = vh_ref[:, columns]
        va_ref[WINDOW:, 2 * c * HD : (2 * c + 1) * HD] = v_ref[:, columns]
        va_ref[:WINDOW, (2 * c + 1) * HD : (2 * c + 2) * HD] = ones
        va_ref[WINDOW:, (2 * c + 1) * HD : (2 * c + 2) * HD] = jnp.ones((local, HD), jnp.bfloat16)

    def halo(t, _):
        at = pl.ds(pl.multiple_of(t * TILE, TILE), TILE)
        for c in range(local_kv):
            columns = slice(c * HD, (c + 1) * HD)
            rows = kh_ref[at, columns].astype(jnp.float32)
            kn_ref[at, columns] = normed(rows, kg_ref[...], cos_ref[at, :], sin_ref[at, :]).astype(jnp.bfloat16)
        return 0

    lax.fori_loop(0, WINDOW // TILE, halo, 0)

    def own(t, _):
        at = pl.ds(pl.multiple_of(t * TILE, TILE), TILE)
        to = pl.ds(pl.multiple_of(t * TILE + WINDOW, TILE), TILE)
        cosine, sine = cos_ref[to, :], sin_ref[to, :]
        for c in range(local_kv):
            columns = slice(c * HD, (c + 1) * HD)
            rows = k_ref[at, columns].astype(jnp.float32)
            kn_ref[to, columns] = normed(rows, kg_ref[...], cosine, sine).astype(jnp.bfloat16)
        for h in range(local_kv * group):
            columns = slice(h * HD, (h + 1) * HD)
            rows = q_ref[at, columns].astype(jnp.float32)
            rows = normed(rows, qg_ref[...], cosine, sine) * QSCALAR ** (-0.5)
            qn_ref[at, columns] = rows.astype(jnp.bfloat16)
        return 0

    lax.fori_loop(0, local // TILE, own, 0)

    span = WINDOW + TILE
    rows_in = lax.broadcasted_iota(jnp.int32, (group * TILE, TILE), 0) % TILE
    columns_in = lax.broadcasted_iota(jnp.int32, (group * TILE, TILE), 1)
    early = columns_in > rows_in
    late = columns_in <= rows_in
    lowest = jnp.where(first_ref[0] == 1, WINDOW, 0)

    def band(t, _):
        at = pl.ds(pl.multiple_of(t * TILE, TILE), TILE)
        keys_at = pl.ds(pl.multiple_of(t * TILE, TILE), span)
        column = lax.broadcasted_iota(jnp.int32, (1, span), 1) + t * TILE
        bias = jnp.where(column >= lowest, 0.0, NEG)
        tops, totals = [], []
        for c in range(local_kv):
            heads = [slice((c * group + g) * HD, (c * group + g + 1) * HD) for g in range(group)]
            query = jnp.concatenate([qn_ref[at, h] for h in heads], axis=0)
            score = dot_t(query, kn_ref[keys_at, c * HD : (c + 1) * HD]) + bias
            score = jnp.concatenate(
                [
                    jnp.where(early, score[:, :TILE], NEG),
                    score[:, TILE:WINDOW],
                    jnp.where(late, score[:, WINDOW:], NEG),
                ],
                axis=1,
            )
            top = jnp.max(score, axis=1, keepdims=True)
            weight = jnp.exp(score - top).astype(jnp.bfloat16)
            out = jnp.dot(
                weight,
                va_ref[keys_at, 2 * c * HD : (2 * c + 2) * HD],
                preferred_element_type=jnp.float32,
            )
            for g, h in enumerate(heads):
                mine = slice(g * TILE, (g + 1) * TILE)
                acc_ref[at, h] = out[mine, :HD]
                tops.append(top[mine])
                totals.append(out[mine, HD:])
        ml_ref[at, :] = pack_state(tops + totals)
        return 0

    lax.fori_loop(0, local // TILE, band, 0)


def prefix_kernel(last, q_ref, acc_in_ref, ml_in_ref, p_ref, *rest):
    if last:
        out_ref, va_ref = rest
    else:
        acc_ref, ml_ref, va_ref = rest
    local = q_ref.shape[0]
    local_kv = p_ref.shape[1] // (2 * HD)
    group = q_ref.shape[1] // HD // local_kv
    tokens = p_ref.shape[0]
    for c in range(local_kv):
        va_ref[:, 2 * c * HD : (2 * c + 1) * HD] = p_ref[:, (2 * c + 1) * HD : (2 * c + 2) * HD]
        va_ref[:, (2 * c + 1) * HD : (2 * c + 2) * HD] = jnp.ones((tokens, HD), jnp.bfloat16)

    def step(t, _):
        at = pl.ds(pl.multiple_of(t * TILE, TILE), TILE)
        state = ml_in_ref[at, :]
        count = local_kv * group
        tops, totals = [], []
        for c in range(local_kv):
            heads = [slice((c * group + g) * HD, (c * group + g + 1) * HD) for g in range(group)]
            query = jnp.concatenate([q_ref[at, h] for h in heads], axis=0)
            before = jnp.concatenate(
                [state[:, c * group + g : c * group + g + 1] for g in range(group)], axis=0
            )
            score = dot_t(query, p_ref[:, 2 * c * HD : (2 * c + 1) * HD])
            top = jnp.maximum(before, jnp.max(score, axis=1, keepdims=True))
            weight = jnp.exp(score - top).astype(jnp.bfloat16)
            out = jnp.dot(
                weight, va_ref[:, 2 * c * HD : (2 * c + 2) * HD], preferred_element_type=jnp.float32
            )
            keep = jnp.exp(before - top)
            for g, h in enumerate(heads):
                mine = slice(g * TILE, (g + 1) * TILE)
                at_head = count + c * group + g
                total = state[:, at_head : at_head + 1] * keep[mine] + out[mine, HD:]
                summed = acc_in_ref[at, h] * keep[mine] + out[mine, :HD]
                if last:
                    out_ref[at, h] = (summed / total).astype(jnp.bfloat16)
                else:
                    acc_ref[at, h] = summed
                    tops.append(top[mine])
                    totals.append(total)
        if not last:
            ml_ref[at, :] = pack_state(tops + totals)
        return 0

    lax.fori_loop(0, local // TILE, step, 0)


WHOLE = pl.BlockSpec(memory_space=pltpu.VMEM)
PARAMS = pltpu.CompilerParams(vmem_limit_bytes=VMEM_LIMIT)


def cost(pairs, in_out):
    return pl.CostEstimate(flops=4 * pairs * HD, transcendentals=pairs, bytes_accessed=in_out)


def band_part(first, q, kh, k, vh, v, q_gain, k_gain, cosine, sine):
    local, width = q.shape
    return pl.pallas_call(
        band_kernel,
        out_shape=(
            jax.ShapeDtypeStruct((local, width), jnp.bfloat16),
            jax.ShapeDtypeStruct((local, width), jnp.float32),
            jax.ShapeDtypeStruct((local, HD), jnp.float32),
        ),
        in_specs=[pl.BlockSpec(memory_space=pltpu.SMEM)] + [WHOLE] * 9,
        out_specs=(WHOLE,) * 3,
        scratch_shapes=[
            pltpu.VMEM((WINDOW + local, k.shape[1]), jnp.bfloat16),
            pltpu.VMEM((WINDOW + local, 2 * k.shape[1]), jnp.bfloat16),
        ],
        compiler_params=PARAMS,
        cost_estimate=cost(local * (width // HD) * (WINDOW + TILE), 12 << 20),
        name="band",
    )(first, q, kh, k, vh, v, q_gain, k_gain, cosine, sine)


def prefix_part(last, q, acc, ml, piece):
    local, width = q.shape
    if last:
        out_shape = jax.ShapeDtypeStruct((local, width), jnp.bfloat16)
        out_specs = WHOLE
    else:
        out_shape = (
            jax.ShapeDtypeStruct((local, width), jnp.float32),
            jax.ShapeDtypeStruct((local, HD), jnp.float32),
        )
        out_specs = (WHOLE,) * 2
    return pl.pallas_call(
        functools.partial(prefix_kernel, last),
        out_shape=out_shape,
        in_specs=[WHOLE] * 4,
        out_specs=out_specs,
        scratch_shapes=[pltpu.VMEM(piece.shape, jnp.bfloat16)],
        compiler_params=PARAMS,
        cost_estimate=cost(local * (width // HD) * piece.shape[0], 12 << 20),
        name="prefix_last" if last else "prefix",
    )(q, acc, ml, piece)


def on_device(queries, keys, values, q_gain, k_gain, positions, prefix_cache, owner):
    local = queries.shape[0]
    seq = lax.axis_index("seq")
    onward = [(i, i + 1) for i in range(lax.axis_size("seq") - 1)]
    keys_before = lax.ppermute(keys[local - WINDOW :], "seq", onward)
    values_before = lax.ppermute(values[local - WINDOW :], "seq", onward)

    mine = scatter_from(prefix_cache[0], owner[0])
    width = mine.shape[1] // lax.axis_size("head")
    mine = lax.all_to_all(mine, "head", split_axis=1, concat_axis=0, tiled=True)
    pieces = [mine] + [round_z(mine, r) for r in ROUNDS]
    gathered = jnp.concatenate(pieces, axis=0)
    gathered = jnp.concatenate([gathered, other_half(gathered)], axis=0)
    sibling = other_core(gathered)

    half = HD // 2
    freq = 10000.0 ** (-(jnp.arange(half).astype(jnp.float32) * 2.0) / HD)
    extended = positions[0] + jnp.arange(-WINDOW, local, dtype=jnp.int32)
    angle = extended.astype(jnp.float32)[:, None] * freq[None, :]
    cosine, sine = jnp.cos(angle), jnp.sin(angle)
    cosine = jnp.concatenate([cosine, cosine], axis=1)
    sine = jnp.concatenate([-sine, sine], axis=1)
    first = (seq == 0).astype(jnp.int32).reshape(1)
    query, acc, ml = band_part(
        first, queries, keys_before, keys, values_before, values,
        (1.0 + q_gain)[None], (1.0 + k_gain)[None], cosine, sine,
    )
    acc, ml = prefix_part(False, query, acc, ml, gathered)
    return prefix_part(True, query, acc, ml, sibling)


def solution(mesh):
    return jax.shard_map(
        on_device,
        mesh=mesh,
        in_specs=(
            P("seq", "head"),
            P("seq", "head"),
            P("seq", "head"),
            P(),
            P(),
            P("seq"),
            P("seq", "head", None),
            P(),
        ),
        out_specs=P("seq", "head"),
        check_vma=False,
    )
```

```python
import functools

import jax
import jax.numpy as jnp
from jax import lax
from jax.experimental import pallas as pl
from jax.experimental.pallas import tpu as pltpu
from jax.sharding import Mesh, PartitionSpec as P

HD = 128
WINDOW = 1024
QSCALAR = 168
YH, NZ, NC, NH = 2, 8, 2, 8
SEQ = ("yh", "z", "core")
BAND_TILE = 256
TILE = 512
CHUNK = 256
NEG = -1e30
BIG = 1e30
VMEM_LIMIT = 36 * 1024 * 1024


def swapped(array, axis):
    return lax.ppermute(array, axis, [(0, 1), (1, 0)])


def round_z(array, r):
    return lax.ppermute(array, "z", [(i, (i + r) % NZ) for i in range(NZ)])


def pick(array, at):
    return lax.dynamic_index_in_dim(array, at, 0, keepdims=False)


def halved(part, axis, root_at):
    at = lax.axis_index(axis)
    part = part.reshape(2, part.shape[0] // 2, part.shape[1])
    came = swapped(pick(part, 1 - at), axis)
    return jnp.where(root_at == at, pick(part, at), came)


def normed(rows, gain, cosine, sine):
    mean_sq = jnp.mean(rows * rows, axis=-1, keepdims=True)
    rows = rows * lax.rsqrt(mean_sq + 1e-06) * gain
    return rows * cosine + pltpu.roll(rows, HD // 2, 1) * sine


def dot_t(a, b):
    return lax.dot_general(a, b, (((1,), (1,)), ((), ())), preferred_element_type=jnp.float32)


def packed(parts):
    lane = lax.broadcasted_iota(jnp.int32, (parts[0].shape[0], HD), 1)
    out = jnp.zeros((parts[0].shape[0], HD), jnp.float32)
    for at, part in enumerate(parts):
        out = jnp.where(lane == at, part, out)
    return out


def rows_at(t, tile):
    return pl.ds(pl.multiple_of(t * tile, tile), tile)


def columns_of(h):
    return slice(h * HD, (h + 1) * HD)


def prep_kernel(q_ref, k_ref, qg_ref, kg_ref, cos_ref, sin_ref, qn_ref, kn_ref):
    local = q_ref.shape[0]

    def own(t, _):
        at = rows_at(t, BAND_TILE)
        cosine, sine = cos_ref[at, :], sin_ref[at, :]
        for c in range(k_ref.shape[1] // HD):
            rows = k_ref[at, columns_of(c)].astype(jnp.float32)
            kn_ref[at, columns_of(c)] = normed(rows, kg_ref[...], cosine, sine).astype(jnp.bfloat16)
        for h in range(q_ref.shape[1] // HD):
            rows = q_ref[at, columns_of(h)].astype(jnp.float32)
            rows = normed(rows, qg_ref[...], cosine, sine) * QSCALAR ** (-0.5)
            qn_ref[at, columns_of(h)] = rows.astype(jnp.bfloat16)
        return 0

    lax.fori_loop(0, local // BAND_TILE, own, 0)


def attend(state, query, key, value, keep_score=None, dead=None):
    score = dot_t(query, key)
    if keep_score is not None:
        score = jnp.where(keep_score, score, NEG)
    top = jnp.max(score, axis=1, keepdims=True)
    if dead is not None:
        top = jnp.where(dead, NEG, top)
    if state is not None:
        top = jnp.maximum(state[0], top)
    minus = top if dead is None else jnp.where(dead, BIG, top)
    weight = jnp.exp(score - minus).astype(jnp.bfloat16)
    out = jnp.dot(weight, value, preferred_element_type=jnp.float32)
    if state is not None:
        out = state[1] * jnp.exp(state[0] - top) + out
    return top, out


def band_kernel(
    first_ref, q_ref, before_ref, k_ref, v_ref, kg_ref, cos_ref, sin_ref,
    acc_ref, ml_ref, ke_ref, va_ref,
):
    local = q_ref.shape[0]
    kv = k_ref.shape[1] // HD
    group = q_ref.shape[1] // HD // kv
    for c in range(kv):
        va_ref[:WINDOW, columns_of(2 * c)] = before_ref[:, columns_of(kv + c)]
        va_ref[WINDOW:, columns_of(2 * c)] = v_ref[:, columns_of(c)]
        va_ref[:, columns_of(2 * c + 1)] = jnp.ones((WINDOW + local, HD), jnp.bfloat16)
    ke_ref[WINDOW:, :] = k_ref[...]

    def halo(t, _):
        at = rows_at(t, BAND_TILE)
        for c in range(kv):
            rows = before_ref[at, columns_of(c)].astype(jnp.float32)
            ke_ref[at, columns_of(c)] = normed(
                rows, kg_ref[...], cos_ref[at, :], sin_ref[at, :]
            ).astype(jnp.bfloat16)
        return 0

    lax.fori_loop(0, WINDOW // BAND_TILE, halo, 0)

    rows_in = lax.broadcasted_iota(jnp.int32, (group * BAND_TILE, CHUNK), 0) % BAND_TILE
    columns_in = lax.broadcasted_iota(jnp.int32, (group * BAND_TILE, CHUNK), 1)
    early = columns_in > rows_in
    late = columns_in <= rows_in
    before_blocks = WINDOW // CHUNK
    is_first = first_ref[0] == 1

    def band(t, _):
        at = rows_at(t, BAND_TILE)
        state = [None] * kv
        for j in range(before_blocks, -1, -1):
            keys_at = rows_at(t + j, CHUNK)
            for c in range(kv):
                query = jnp.concatenate(
                    [q_ref[at, columns_of(c * group + g)] for g in range(group)], axis=0
                )
                state[c] = attend(
                    state[c],
                    query,
                    ke_ref[keys_at, columns_of(c)],
                    va_ref[keys_at, 2 * c * HD : (2 * c + 2) * HD],
                    keep_score=late if j == before_blocks else early if j == 0 else None,
                    dead=None if j == before_blocks else is_first & (t + j < before_blocks),
                )
        tops, totals = [], []
        for c in range(kv):
            for g in range(group):
                mine = slice(g * BAND_TILE, (g + 1) * BAND_TILE)
                acc_ref[at, columns_of(c * group + g)] = state[c][1][mine, :HD]
                tops.append(state[c][0][mine])
                totals.append(state[c][1][mine, HD:])
        ml_ref[at, :] = packed(tops + totals)
        return 0

    lax.fori_loop(0, local // BAND_TILE, band, 0)


def prefix_kernel(last, pieces, q_ref, acc_in_ref, ml_in_ref, *rest):
    p_refs, rest = rest[:pieces], rest[pieces:]
    if last:
        out_ref, va_ref = rest
    else:
        acc_ref, ml_ref, va_ref = rest
    local = q_ref.shape[0]
    tokens = p_refs[0].shape[0]
    kv = p_refs[0].shape[1] // (2 * HD)
    group = q_ref.shape[1] // HD // kv
    for c in range(kv):
        for i, p_ref in enumerate(p_refs):
            va_ref[i * tokens : (i + 1) * tokens, columns_of(2 * c)] = p_ref[:, columns_of(2 * c + 1)]
        va_ref[:, columns_of(2 * c + 1)] = jnp.ones((pieces * tokens, HD), jnp.bfloat16)

    def step(t, _):
        at = rows_at(t, TILE)
        count = kv * group
        queries, state = [], []
        for c in range(kv):
            heads = range(c * group, (c + 1) * group)
            queries.append(jnp.concatenate([q_ref[at, columns_of(h)] for h in heads], axis=0))
            top = jnp.concatenate([ml_in_ref[at, h : h + 1] for h in heads], axis=0)
            total = jnp.concatenate([ml_in_ref[at, count + h : count + h + 1] for h in heads], axis=0)
            summed = jnp.concatenate([acc_in_ref[at, columns_of(h)] for h in heads], axis=0)
            both = jnp.concatenate([summed, jnp.broadcast_to(total, summed.shape)], axis=1)
            state.append((top, both))
        for i, p_ref in enumerate(p_refs):
            for j in range(tokens // CHUNK):
                at_keys = slice(j * CHUNK, (j + 1) * CHUNK)
                at_values = slice(i * tokens + j * CHUNK, i * tokens + (j + 1) * CHUNK)
                for c in range(kv):
                    state[c] = attend(
                        state[c],
                        queries[c],
                        p_ref[at_keys, columns_of(2 * c)],
                        va_ref[at_values, 2 * c * HD : (2 * c + 2) * HD],
                    )
        tops, totals = [], []
        for c in range(kv):
            top, both = state[c]
            if last:
                both = (both[:, :HD] / both[:, HD:]).astype(jnp.bfloat16)
            for g in range(group):
                mine = slice(g * TILE, (g + 1) * TILE)
                if last:
                    out_ref[at, columns_of(c * group + g)] = both[mine]
                else:
                    acc_ref[at, columns_of(c * group + g)] = both[mine, :HD]
                    tops.append(top[mine])
                    totals.append(both[mine, HD:])
        if not last:
            ml_ref[at, :] = packed(tops + totals)
        return 0

    lax.fori_loop(0, local // TILE, step, 0)


WHOLE = pl.BlockSpec(memory_space=pltpu.VMEM)
PARAMS = pltpu.CompilerParams(vmem_limit_bytes=VMEM_LIMIT)


def cost(pairs, in_out):
    return pl.CostEstimate(flops=8 * pairs * HD, transcendentals=pairs, bytes_accessed=in_out)


def prep(q, k, q_gain, k_gain, cosine, sine):
    return pl.pallas_call(
        prep_kernel,
        out_shape=(
            jax.ShapeDtypeStruct(q.shape, jnp.bfloat16),
            jax.ShapeDtypeStruct(k.shape, jnp.bfloat16),
        ),
        in_specs=[WHOLE] * 6,
        out_specs=(WHOLE,) * 2,
        compiler_params=PARAMS,
        cost_estimate=pl.CostEstimate(flops=40 * q.size, transcendentals=q.shape[0] * 6, bytes_accessed=8 << 20),
        name="prep",
    )(q, k, q_gain, k_gain, cosine, sine)


def band_part(first, q, before, k, v, k_gain, cosine, sine):
    local, width = q.shape
    return pl.pallas_call(
        band_kernel,
        out_shape=(
            jax.ShapeDtypeStruct((local, width), jnp.float32),
            jax.ShapeDtypeStruct((local, HD), jnp.float32),
        ),
        in_specs=[pl.BlockSpec(memory_space=pltpu.SMEM)] + [WHOLE] * 7,
        out_specs=(WHOLE,) * 2,
        scratch_shapes=[
            pltpu.VMEM((WINDOW + local, k.shape[1]), jnp.bfloat16),
            pltpu.VMEM((WINDOW + local, 2 * k.shape[1]), jnp.bfloat16),
        ],
        compiler_params=PARAMS,
        cost_estimate=cost(local * (width // HD) * (WINDOW + BAND_TILE), 10 << 20),
        name="band",
    )(first, q, before, k, v, k_gain, cosine, sine)


def prefix_part(last, q, acc, ml, *pieces):
    local, width = q.shape
    rows, columns = pieces[0].shape
    if last:
        out_shape = jax.ShapeDtypeStruct((local, width), jnp.bfloat16)
        out_specs = WHOLE
    else:
        out_shape = (
            jax.ShapeDtypeStruct((local, width), jnp.float32),
            jax.ShapeDtypeStruct((local, HD), jnp.float32),
        )
        out_specs = (WHOLE,) * 2
    return pl.pallas_call(
        functools.partial(prefix_kernel, last, len(pieces)),
        out_shape=out_shape,
        in_specs=[WHOLE] * (3 + len(pieces)),
        out_specs=out_specs,
        scratch_shapes=[pltpu.VMEM((len(pieces) * rows, columns), jnp.bfloat16)],
        compiler_params=PARAMS,
        cost_estimate=cost(local * (width // HD) * len(pieces) * rows, 10 << 20),
        name="prefix_last" if last else "prefix",
    )(q, acc, ml, *pieces)


def on_device(queries, keys, values, q_gain, k_gain, positions, prefix_cache, owner):
    local = queries.shape[0]
    root = owner[0]
    root_y, root_z, root_c = root // (NZ * NC), (root // NC) % NZ, root % NC

    slab = halved(prefix_cache[0], "core", root_c)
    onward = [(i, i + 1) for i in range(YH * NZ * NC - 1)]
    tail = jnp.concatenate([keys[local - WINDOW :], values[local - WINDOW :]], axis=1)
    slab, tail = lax.optimization_barrier((slab, tail))
    before = lax.ppermute(tail, SEQ, onward)
    slab = halved(slab, "yh", root_y)

    half = HD // 2
    freq = 10000.0 ** (-(jnp.arange(half).astype(jnp.float32) * 2.0) / HD)
    extended = positions[0] + jnp.arange(-WINDOW, local, dtype=jnp.int32)
    angle = extended.astype(jnp.float32)[:, None] * freq[None, :]
    cosine, sine = jnp.cos(angle), jnp.sin(angle)
    cosine = jnp.concatenate([cosine, cosine], axis=1)
    sine = jnp.concatenate([-sine, sine], axis=1)
    cosine, sine, slab = lax.optimization_barrier((cosine, sine, slab))

    rows, wide = slab.shape
    parts = slab.reshape(NZ, rows // NZ, NH, wide // NH).transpose(0, 2, 1, 3)
    parts = parts.reshape(NZ * NH, rows // NZ, wide // NH)
    parts = lax.all_to_all(parts, ("z", "head"), split_axis=0, concat_axis=0, tiled=True)
    query, key = prep(
        queries, keys, (1.0 + q_gain)[None], (1.0 + k_gain)[None], cosine[WINDOW:], sine[WINDOW:]
    )
    first = (lax.axis_index(SEQ) == 0).astype(jnp.int32).reshape(1)
    acc, ml = band_part(
        first, query, before, key, values, (1.0 + k_gain)[None], cosine[:WINDOW], sine[:WINDOW]
    )
    mine = pick(parts.reshape(NZ, NH, rows // NZ, wide // NH), root_z)
    mine = mine.reshape(NH * rows // NZ, wide // NH)
    mine, ml = lax.optimization_barrier((mine, ml))

    mine = jnp.concatenate([mine, round_z(mine, NZ // 2)], axis=0)
    mine = jnp.concatenate([mine, round_z(mine, 1), round_z(mine, -1), round_z(mine, 2)], axis=0)
    far = swapped(mine, "yh")
    acc, ml = prefix_part(False, query, acc, ml, mine, swapped(mine, "core"))
    far, ml = lax.optimization_barrier((far, ml))
    last = swapped(far, "core")
    acc, ml = prefix_part(False, query, acc, ml, far)
    return prefix_part(True, query, acc, ml, last)


def solution(mesh):
    fine = Mesh(mesh.devices.reshape(YH, NZ, NC, NH), SEQ + ("head",))
    return jax.shard_map(
        on_device,
        mesh=fine,
        in_specs=(
            P(SEQ, "head"),
            P(SEQ, "head"),
            P(SEQ, "head"),
            P(),
            P(),
            P(SEQ),
            P(SEQ, "head", None),
            P(),
        ),
        out_specs=P(SEQ, "head"),
        check_vma=False,
    )
```

```python
import functools

import jax
import jax.numpy as jnp
from jax import lax
from jax.experimental import pallas as pl
from jax.experimental.pallas import tpu as pltpu
from jax.sharding import Mesh, PartitionSpec as P

HD = 128
WINDOW = 1024
QSCALAR = 168
YH, NZ, NC, NH = 2, 8, 2, 8
SEQ = ("yh", "z", "core")
BAND_TILE = 256
TILE = 512
CHUNK = 256
NEG = -1e30
BIG = 1e30
VMEM_LIMIT = 24 * 1024 * 1024


def swapped(array, axis):
    return lax.ppermute(array, axis, [(0, 1), (1, 0)])


def round_z(array, r):
    return lax.ppermute(array, "z", [(i, (i + r) % NZ) for i in range(NZ)])


def pick(array, at):
    return lax.dynamic_index_in_dim(array, at, 0, keepdims=False)


def halved(part, axis, root_at):
    at = lax.axis_index(axis)
    part = part.reshape(2, part.shape[0] // 2, part.shape[1])
    came = swapped(pick(part, 1 - at), axis)
    return jnp.where(root_at == at, pick(part, at), came)


def normed(rows, gain, cosine, sine):
    mean_sq = jnp.mean(rows * rows, axis=-1, keepdims=True)
    rows = rows * lax.rsqrt(mean_sq + 1e-06) * gain
    return rows * cosine + pltpu.roll(rows, HD // 2, 1) * sine


def tables(cos_ref, sin_ref, at):
    cosine, sine = cos_ref[at, :], sin_ref[at, :]
    return jnp.concatenate([cosine, cosine], axis=1), jnp.concatenate([-sine, sine], axis=1)


def dot_t(a, b):
    return lax.dot_general(a, b, (((1,), (1,)), ((), ())), preferred_element_type=jnp.float32)


def rows_at(t, tile):
    return pl.ds(pl.multiple_of(t * tile, tile), tile)


def columns_of(h):
    return slice(h * HD, (h + 1) * HD)


def stacked(ref, at, heads):
    return jnp.concatenate([ref[at, columns_of(h)] for h in heads], axis=0)


def prep_kernel(q_ref, k_ref, qg_ref, kg_ref, cos_ref, sin_ref, qn_ref, kn_ref):
    local = q_ref.shape[0]

    def own(t, _):
        at = rows_at(t, BAND_TILE)
        cosine, sine = tables(cos_ref, sin_ref, rows_at(t + WINDOW // BAND_TILE, BAND_TILE))
        for c in range(k_ref.shape[1] // HD):
            rows = k_ref[at, columns_of(c)].astype(jnp.float32)
            kn_ref[at, columns_of(c)] = normed(rows, kg_ref[...], cosine, sine).astype(jnp.bfloat16)
        for h in range(q_ref.shape[1] // HD):
            rows = q_ref[at, columns_of(h)].astype(jnp.float32)
            rows = normed(rows, qg_ref[...], cosine, sine) * QSCALAR ** (-0.5)
            qn_ref[at, columns_of(h)] = rows.astype(jnp.bfloat16)
        return 0

    lax.fori_loop(0, local // BAND_TILE, own, 0)


def halo_kernel(k_ref, kg_ref, cos_ref, sin_ref, kn_ref):
    def one(t, _):
        at = rows_at(t, BAND_TILE)
        cosine, sine = tables(cos_ref, sin_ref, at)
        for c in range(kn_ref.shape[1] // HD):
            rows = k_ref[at, columns_of(c)].astype(jnp.float32)
            kn_ref[at, columns_of(c)] = normed(rows, kg_ref[...], cosine, sine).astype(jnp.bfloat16)
        return 0

    lax.fori_loop(0, WINDOW // BAND_TILE, one, 0)


def attend(state, query, key, value, keep_score=None, dead=None):
    score = dot_t(query, key)
    if keep_score is not None:
        score = jnp.where(keep_score, score, NEG)
    top = jnp.max(score, axis=1, keepdims=True)
    if dead is not None:
        top = jnp.where(dead, NEG, top)
    top = jnp.broadcast_to(top, query.shape)
    if state is not None:
        top = jnp.maximum(state[0], top)
    minus = top if dead is None else jnp.where(dead, BIG, top)
    weight = jnp.concatenate(
        [jnp.exp(score[:, i : i + HD] - minus).astype(jnp.bfloat16) for i in range(0, score.shape[1], HD)],
        axis=1,
    )
    value = jnp.concatenate([value, jnp.ones_like(value)], axis=1)
    out = jnp.dot(weight, value, preferred_element_type=jnp.float32)
    summed, total = out[:, :HD], out[:, HD:]
    if state is not None:
        keep = jnp.exp(state[0] - top)
        summed, total = state[1] * keep + summed, state[2] * keep + total
    return top, summed, total


def band_kernel(from_tile, first_ref, q_ref, kb_ref, vb_ref, k_ref, v_ref, top_ref, acc_ref, sum_ref):
    kv = k_ref.shape[1] // HD
    group = q_ref.shape[1] // HD // kv
    rows_in = lax.broadcasted_iota(jnp.int32, (group * BAND_TILE, CHUNK), 0) % BAND_TILE
    columns_in = lax.broadcasted_iota(jnp.int32, (group * BAND_TILE, CHUNK), 1)
    early = columns_in > rows_in
    late = columns_in <= rows_in
    reach = WINDOW // CHUNK
    is_first = first_ref[0] == 1
    for t in range(top_ref.shape[0] // BAND_TILE):
        block = from_tile + t
        at = slice(block * BAND_TILE, (block + 1) * BAND_TILE)
        to = slice(t * BAND_TILE, (t + 1) * BAND_TILE)
        queries = [stacked(q_ref, at, range(c * group, (c + 1) * group)) for c in range(kv)]
        state = [None] * kv
        for j in range(reach, -1, -1):
            e = block + j - reach
            mine = e >= 0
            keys_at = slice(e * CHUNK, (e + 1) * CHUNK) if mine else slice((e + reach) * CHUNK, (e + reach + 1) * CHUNK)
            for c in range(kv):
                state[c] = attend(
                    state[c],
                    queries[c],
                    (k_ref if mine else kb_ref)[keys_at, columns_of(c)],
                    v_ref[keys_at, columns_of(c)] if mine else vb_ref[keys_at, columns_of(kv + c)],
                    keep_score=late if j == reach else early if j == 0 else None,
                    dead=None if mine else is_first,
                )
        for c in range(kv):
            for g in range(group):
                rows = slice(g * BAND_TILE, (g + 1) * BAND_TILE)
                for ref, part in zip((top_ref, acc_ref, sum_ref), state[c]):
                    ref[to, columns_of(c * group + g)] = part[rows]


def prefix_kernel(last, bands, pieces, q_ref, *rest):
    states, rest = [rest[3 * i : 3 * i + 3] for i in range(bands)], rest[3 * bands :]
    p_refs, outs = rest[:pieces], rest[pieces:]
    tokens = p_refs[0].shape[0]
    kv = p_refs[0].shape[1] // (2 * HD)
    group = q_ref.shape[1] // HD // kv
    each = states[0][0].shape[0]

    def step(t, state_refs, at_in):
        at = rows_at(t, TILE)
        heads = [range(c * group, (c + 1) * group) for c in range(kv)]
        queries = [stacked(q_ref, at, heads[c]) for c in range(kv)]
        state = [tuple(stacked(ref, at_in, heads[c]) for ref in state_refs) for c in range(kv)]
        for p_ref in p_refs:
            for j in range(tokens // CHUNK):
                at_keys = slice(j * CHUNK, (j + 1) * CHUNK)
                for c in range(kv):
                    state[c] = attend(
                        state[c],
                        queries[c],
                        p_ref[at_keys, columns_of(2 * c)],
                        p_ref[at_keys, columns_of(2 * c + 1)],
                    )
        for c in range(kv):
            result = [(state[c][1] / state[c][2]).astype(jnp.bfloat16)] if last else state[c]
            for g in range(group):
                rows = slice(g * TILE, (g + 1) * TILE)
                for ref, part in zip(outs, result):
                    ref[at, columns_of(c * group + g)] = part[rows]

    if bands > 1:
        for i in range(q_ref.shape[0] // TILE):
            step(i, states[i * TILE // each], slice(i * TILE % each, i * TILE % each + TILE))
    else:

        def one(t, _):
            step(t, states[0], rows_at(t, TILE))
            return 0

        lax.fori_loop(0, q_ref.shape[0] // TILE, one, 0)


WHOLE = pl.BlockSpec(memory_space=pltpu.VMEM)
PARAMS = pltpu.CompilerParams(vmem_limit_bytes=VMEM_LIMIT)


def cost(pairs, in_out):
    return pl.CostEstimate(flops=8 * pairs * HD, transcendentals=pairs, bytes_accessed=in_out)


def normed_part(kernel, outs, *args):
    size = sum(o.size for o in outs)
    return pl.pallas_call(
        kernel,
        out_shape=outs,
        in_specs=[WHOLE] * len(args),
        out_specs=(WHOLE,) * len(outs),
        compiler_params=PARAMS,
        cost_estimate=pl.CostEstimate(flops=60 * size, transcendentals=size // HD, bytes_accessed=6 * size),
        name="norm_rope",
    )(*args)


def band_part(from_tile, tiles, first, q, key_before, before, k, v):
    width = q.shape[1]
    rows = tiles * BAND_TILE
    return pl.pallas_call(
        functools.partial(band_kernel, from_tile),
        out_shape=(jax.ShapeDtypeStruct((rows, width), jnp.float32),) * 3,
        in_specs=[pl.BlockSpec(memory_space=pltpu.SMEM)] + [WHOLE] * 5,
        out_specs=(WHOLE,) * 3,
        compiler_params=PARAMS,
        cost_estimate=cost(rows * (width // HD) * (WINDOW + BAND_TILE), 6 << 20),
        name="band",
    )(first, q, key_before, before, k, v)


def prefix_part(last, q, states, *pieces):
    local, width = q.shape
    flat = [part for state in states for part in state]
    if last:
        out_shape = jax.ShapeDtypeStruct((local, width), jnp.bfloat16)
        out_specs = WHOLE
    else:
        out_shape = (jax.ShapeDtypeStruct((local, width), jnp.float32),) * 3
        out_specs = (WHOLE,) * 3
    return pl.pallas_call(
        functools.partial(prefix_kernel, last, len(states), len(pieces)),
        out_shape=out_shape,
        in_specs=[WHOLE] * (1 + len(flat) + len(pieces)),
        out_specs=out_specs,
        compiler_params=PARAMS,
        cost_estimate=cost(local * (width // HD) * len(pieces) * pieces[0].shape[0], 10 << 20),
        name="prefix_last" if last else "prefix",
    )(q, *flat, *pieces)


def on_device(queries, keys, values, q_gain, k_gain, positions, prefix_cache, owner):
    local = queries.shape[0]
    root = owner[0]
    root_y, root_z, root_c = root // (NZ * NC), (root // NC) % NZ, root % NC
    q_gain, k_gain = (1.0 + q_gain)[None], (1.0 + k_gain)[None]
    first = (lax.axis_index(SEQ) == 0).astype(jnp.int32).reshape(1)

    slab = halved(prefix_cache[0], "core", root_c)
    onward = [(i, i + 1) for i in range(YH * NZ * NC - 1)]
    tail = jnp.concatenate([keys[local - WINDOW :], values[local - WINDOW :]], axis=1)
    slab, tail = lax.optimization_barrier((slab, tail))
    before = lax.ppermute(tail, SEQ, onward)
    slab = halved(slab, "yh", root_y)

    half = HD // 2
    freq = 10000.0 ** (-(jnp.arange(half).astype(jnp.float32) * 2.0) / HD)
    extended = positions[0] + jnp.arange(-WINDOW, local, dtype=jnp.int32)
    angle = extended.astype(jnp.float32)[:, None] * freq[None, :]
    cosine, sine = jnp.cos(angle), jnp.sin(angle)
    query, key = normed_part(
        prep_kernel,
        (
            jax.ShapeDtypeStruct(queries.shape, jnp.bfloat16),
            jax.ShapeDtypeStruct(keys.shape, jnp.bfloat16),
        ),
        queries, keys, q_gain, k_gain, cosine, sine,
    )
    slab, query = lax.optimization_barrier((slab, query))

    rows, wide = slab.shape
    parts = slab.reshape(NZ, rows // NZ, NH, wide // NH).transpose(0, 2, 1, 3)
    parts = parts.reshape(NZ * NH, rows // NZ, wide // NH)
    parts = lax.all_to_all(parts, ("z", "head"), split_axis=0, concat_axis=0, tiled=True)
    (key_before,) = normed_part(
        halo_kernel,
        (jax.ShapeDtypeStruct((WINDOW, keys.shape[1]), jnp.bfloat16),),
        before, k_gain, cosine, sine,
    )

    def band(at, first):
        return band_part(2 * at, 2, first, query, key_before, before, key, values)

    states = [band(0, first)]
    parts, top = lax.optimization_barrier((parts, states[0][0]))
    states[0] = (top, *states[0][1:])
    mine = pick(parts.reshape(NZ, NH, rows // NZ, wide // NH), root_z)
    mine = mine.reshape(NH * rows // NZ, wide // NH)
    mine, first = lax.optimization_barrier((mine, first))

    across = round_z(mine, NZ // 2)
    states.append(band(1, first))
    across, top = lax.optimization_barrier((across, states[1][0]))
    states[1] = (top, *states[1][1:])
    mine = jnp.concatenate([mine, across], axis=0)
    mine, first = lax.optimization_barrier((mine, first))

    around = [round_z(mine, 1), round_z(mine, -1), round_z(mine, 2)]
    states.append(band(2, first))
    around, top = lax.optimization_barrier((around, states[2][0]))
    states[2] = (top, *states[2][1:])
    mine = jnp.concatenate([mine, *around], axis=0)

    far = swapped(mine, "yh")
    state = prefix_part(False, query, states, mine, swapped(mine, "core"))
    far, top = lax.optimization_barrier((far, state[0]))
    last = swapped(far, "core")
    state = prefix_part(False, query, [(top, *state[1:])], far)
    return prefix_part(True, query, [state], last)


def solution(mesh):
    fine = Mesh(mesh.devices.reshape(YH, NZ, NC, NH), SEQ + ("head",))
    return jax.shard_map(
        on_device,
        mesh=fine,
        in_specs=(
            P(SEQ, "head"),
            P(SEQ, "head"),
            P(SEQ, "head"),
            P(),
            P(),
            P(SEQ),
            P(SEQ, "head", None),
            P(),
        ),
        out_specs=P(SEQ, "head"),
        check_vma=False,
    )
```

```python
import functools

import jax
import jax.numpy as jnp
from jax import lax
from jax.experimental import pallas as pl
from jax.experimental.pallas import tpu as pltpu
from jax.sharding import Mesh, PartitionSpec as P

HD = 128
WINDOW = 1024
QSCALAR = 168
YH, NZ, NC, NH = 2, 8, 2, 8
SEQ = ("yh", "z", "core")
BAND_TILE = 256
TILE = 512
CHUNK = 256
NEG = -1e30
BIG = 1e30
VMEM_LIMIT = 24 * 1024 * 1024


def swapped(array, axis):
    return lax.ppermute(array, axis, [(0, 1), (1, 0)])


def round_z(array, r):
    return lax.ppermute(array, "z", [(i, (i + r) % NZ) for i in range(NZ)])


def pick(array, at):
    return lax.dynamic_index_in_dim(array, at, 0, keepdims=False)


def tables(cos_ref, sin_ref, at, gain, scale):
    cosine, sine = cos_ref[at, :], sin_ref[at, :]
    cosine = jnp.concatenate([cosine, cosine], axis=1)
    sine = jnp.concatenate([-sine, sine], axis=1)
    return cosine * (gain * scale), sine * (pltpu.roll(gain, HD // 2, 1) * scale)


def normed(rows, direct, crossed):
    wide = rows.astype(jnp.float32)
    square = wide * wide
    high = square.astype(jnp.bfloat16)
    low = (square - high.astype(jnp.float32)).astype(jnp.bfloat16)
    even = jnp.full((HD, HD), 1.0 / HD, jnp.bfloat16)
    mean_sq = jnp.dot(high, even, preferred_element_type=jnp.float32)
    mean_sq = mean_sq + jnp.dot(low, even, preferred_element_type=jnp.float32)
    other = pltpu.roll(rows, HD // 2, 1).astype(jnp.float32)
    return ((wide * direct + other * crossed) * lax.rsqrt(mean_sq + 1e-06)).astype(jnp.bfloat16)


def dot_t(a, b):
    return lax.dot_general(a, b, (((1,), (1,)), ((), ())), preferred_element_type=jnp.float32)


def rows_at(t, tile):
    return pl.ds(pl.multiple_of(t * tile, tile), tile)


def columns_of(h):
    return slice(h * HD, (h + 1) * HD)


def stacked(ref, at, heads):
    return jnp.concatenate([ref[at, columns_of(h)] for h in heads], axis=0)


def prep_kernel(q_ref, k_ref, qg_ref, kg_ref, cos_ref, sin_ref, qn_ref, kn_ref):
    def own(t, _):
        at = rows_at(t, BAND_TILE)
        at_table = rows_at(t + WINDOW // BAND_TILE, BAND_TILE)
        q_tables = tables(cos_ref, sin_ref, at_table, qg_ref[...], QSCALAR ** (-0.5))
        k_tables = tables(cos_ref, sin_ref, at_table, kg_ref[...], 1.0)
        for c in range(k_ref.shape[1] // HD):
            kn_ref[at, columns_of(c)] = normed(k_ref[at, columns_of(c)], *k_tables)
        for h in range(q_ref.shape[1] // HD):
            qn_ref[at, columns_of(h)] = normed(q_ref[at, columns_of(h)], *q_tables)
        return 0

    lax.fori_loop(0, q_ref.shape[0] // BAND_TILE, own, 0)


def halo_kernel(k_ref, kg_ref, cos_ref, sin_ref, kn_ref):
    def one(t, _):
        at = rows_at(t, BAND_TILE)
        k_tables = tables(cos_ref, sin_ref, at, kg_ref[...], 1.0)
        for c in range(kn_ref.shape[1] // HD):
            kn_ref[at, columns_of(c)] = normed(k_ref[at, columns_of(c)], *k_tables)
        return 0

    lax.fori_loop(0, WINDOW // BAND_TILE, one, 0)


def attend(state, query, key, value, keep_score=None, dead=None):
    score = dot_t(query, key)
    if keep_score is not None:
        score = jnp.where(keep_score, score, NEG)
    top = jnp.max(score, axis=1, keepdims=True)
    if dead is not None:
        top = jnp.where(dead, NEG, top)
    top = jnp.broadcast_to(top, query.shape)
    if state is not None:
        top = jnp.maximum(state[0], top)
    minus = top if dead is None else jnp.where(dead, BIG, top)
    weight = jnp.concatenate(
        [jnp.exp(score[:, i : i + HD] - minus).astype(jnp.bfloat16) for i in range(0, score.shape[1], HD)],
        axis=1,
    )
    value = jnp.concatenate([value, jnp.ones_like(value)], axis=1)
    out = jnp.dot(weight, value, preferred_element_type=jnp.float32)
    summed, total = out[:, :HD], out[:, HD:]
    if state is not None:
        keep = jnp.exp(state[0] - top)
        summed, total = state[1] * keep + summed, state[2] * keep + total
    return top, summed, total


def band_kernel(part, halo_rows, first_ref, q_ref, k_ref, v_ref, *rest):
    kb_ref, vb_ref = rest[:2] if halo_rows else (None, None)
    outs = rest[-3:]
    kv = k_ref.shape[1] // HD
    group = q_ref.shape[1] // HD // kv
    rows_in = lax.broadcasted_iota(jnp.int32, (group * BAND_TILE, CHUNK), 0) % BAND_TILE
    columns_in = lax.broadcasted_iota(jnp.int32, (group * BAND_TILE, CHUNK), 1)
    early = columns_in > rows_in
    late = columns_in <= rows_in
    reach = WINDOW // CHUNK
    is_first = first_ref[0] == 1
    tiles = q_ref.shape[0] // BAND_TILE
    for t in range(tiles):
        at = slice(t * BAND_TILE, (t + 1) * BAND_TILE)
        queries = [stacked(q_ref, at, range(c * group, (c + 1) * group)) for c in range(kv)]
        state = [None] * kv
        for j in range(reach, -1, -1):
            e = part * tiles + t + j - reach
            mine = e >= 0
            start = e * CHUNK if mine else halo_rows + e * CHUNK
            keys_at = slice(start, start + CHUNK)
            for c in range(kv):
                state[c] = attend(
                    state[c],
                    queries[c],
                    (k_ref if mine else kb_ref)[keys_at, columns_of(c)],
                    (v_ref if mine else vb_ref)[keys_at, columns_of(c)],
                    keep_score=late if j == reach else early if j == 0 else None,
                    dead=None if mine else is_first,
                )
        for c in range(kv):
            for g in range(group):
                rows = slice(g * BAND_TILE, (g + 1) * BAND_TILE)
                for ref, value in zip(outs, state[c]):
                    ref[at, columns_of(c * group + g)] = value[rows]


def blocks_of(p_refs):
    blocks, held, room = [], [], CHUNK
    for p_ref in p_refs:
        start = 0
        while start < p_ref.shape[0]:
            rows = min(room, p_ref.shape[0] - start)
            held.append((p_ref, start, rows))
            start, room = start + rows, room - rows
            if room == 0:
                blocks.append(held)
                held, room = [], CHUNK
    if held and blocks and CHUNK - room < CHUNK:
        blocks[-1] = blocks[-1] + held
    elif held:
        blocks.append(held)
    return blocks


def joined(block, h):
    parts = [p_ref[start : start + rows, columns_of(h)] for p_ref, start, rows in block]
    return parts[0] if len(parts) == 1 else jnp.concatenate(parts, axis=0)


def prefix_kernel(last, bands, pieces, q_ref, *rest):
    states, rest = [rest[3 * i : 3 * i + 3] for i in range(bands)], rest[3 * bands :]
    p_refs, outs = rest[:pieces], rest[pieces:]
    kv = p_refs[0].shape[1] // (2 * HD)
    group = q_ref.shape[1] // HD // kv
    each = states[0][0].shape[0]

    def step(t, state_refs, at_in):
        at = rows_at(t, TILE)
        heads = [range(c * group, (c + 1) * group) for c in range(kv)]
        queries = [stacked(q_ref, at, heads[c]) for c in range(kv)]
        state = [tuple(stacked(ref, at_in, heads[c]) for ref in state_refs) for c in range(kv)]
        for block in blocks_of(p_refs):
            for c in range(kv):
                state[c] = attend(state[c], queries[c], joined(block, 2 * c), joined(block, 2 * c + 1))
        for c in range(kv):
            result = [(state[c][1] / state[c][2]).astype(jnp.bfloat16)] if last else state[c]
            for g in range(group):
                rows = slice(g * TILE, (g + 1) * TILE)
                for ref, part in zip(outs, result):
                    ref[at, columns_of(c * group + g)] = part[rows]

    if bands > 1:
        for i in range(q_ref.shape[0] // TILE):
            step(i, states[i * TILE // each], slice(i * TILE % each, i * TILE % each + TILE))
    else:

        def one(t, _):
            step(t, states[0], rows_at(t, TILE))
            return 0

        lax.fori_loop(0, q_ref.shape[0] // TILE, one, 0)


WHOLE = pl.BlockSpec(memory_space=pltpu.VMEM)
PARAMS = pltpu.CompilerParams(vmem_limit_bytes=VMEM_LIMIT)


def cost(pairs, in_out):
    return pl.CostEstimate(flops=8 * pairs * HD, transcendentals=pairs, bytes_accessed=in_out)


def normed_part(kernel, outs, *args):
    size = sum(o.size for o in outs)
    return pl.pallas_call(
        kernel,
        out_shape=outs,
        in_specs=[WHOLE] * len(args),
        out_specs=(WHOLE,) * len(outs),
        compiler_params=PARAMS,
        cost_estimate=pl.CostEstimate(flops=60 * size, transcendentals=size // HD, bytes_accessed=6 * size),
        name="norm_rope",
    )(*args)


def band_part(part, parts, first, q, k, v, key_before, before):
    width, wide = q.shape[1], k.shape[1]
    rows = q.shape[0] // parts
    halo_rows = max(0, WINDOW - part * rows)
    own = pl.BlockSpec(((part + 1) * rows, wide), lambda i: (0, 0))
    operands = [first, q, k, v]
    in_specs = [
        pl.BlockSpec(memory_space=pltpu.SMEM),
        pl.BlockSpec((rows, width), lambda i: (part, 0)),
        own,
        own,
    ]
    if halo_rows:
        at = WINDOW // halo_rows - 1
        operands += [key_before, before]
        in_specs += [
            pl.BlockSpec((halo_rows, wide), lambda i: (at, 0)),
            pl.BlockSpec((halo_rows, wide), lambda i: (at, 1)),
        ]
    return pl.pallas_call(
        functools.partial(band_kernel, part, halo_rows),
        grid=(1,),
        out_shape=(jax.ShapeDtypeStruct((rows, width), jnp.float32),) * 3,
        in_specs=in_specs,
        out_specs=(WHOLE,) * 3,
        compiler_params=PARAMS,
        cost_estimate=cost(rows * (width // HD) * (WINDOW + BAND_TILE), 5 << 20),
        name="band",
    )(*operands)


def prefix_part(last, q, states, *pieces):
    local, width = q.shape
    flat = [part for state in states for part in state]
    if last:
        out_shape = jax.ShapeDtypeStruct((local, width), jnp.bfloat16)
        out_specs = WHOLE
    else:
        out_shape = (jax.ShapeDtypeStruct((local, width), jnp.float32),) * 3
        out_specs = (WHOLE,) * 3
    return pl.pallas_call(
        functools.partial(prefix_kernel, last, len(states), len(pieces)),
        out_shape=out_shape,
        in_specs=[WHOLE] * (1 + len(flat) + len(pieces)),
        out_specs=out_specs,
        compiler_params=PARAMS,
        cost_estimate=cost(local * (width // HD) * sum(p.shape[0] for p in pieces), 10 << 20),
        name="prefix_last" if last else "prefix",
    )(q, *flat, *pieces)


def on_device(queries, keys, values, q_gain, k_gain, positions, prefix_cache, owner):
    local = queries.shape[0]
    root = owner[0]
    root_y, root_z, root_c = root // (NZ * NC), (root // NC) % NZ, root % NC
    q_gain, k_gain = (1.0 + q_gain)[None], (1.0 + k_gain)[None]
    first = (lax.axis_index(SEQ) == 0).astype(jnp.int32).reshape(1)

    whole = prefix_cache[0]
    siblings = swapped(whole, "core")
    onward = [(i, i + 1) for i in range(YH * NZ * NC - 1)]
    tail = jnp.concatenate([keys[local - WINDOW :], values[local - WINDOW :]], axis=1)
    before = lax.ppermute(tail, SEQ, onward)
    core, y = lax.axis_index("core"), lax.axis_index("yh")

    def quarter(of_y):
        parts = [pick(a.reshape(NC * YH, -1, a.shape[1]), core * YH + of_y) for a in (whole, siblings)]
        return jnp.where(root_c == core, *parts)

    came = swapped(quarter(1 - y), "yh")
    slab = jnp.where(root_y == y, quarter(y), came)

    half = HD // 2
    freq = 10000.0 ** (-(jnp.arange(half).astype(jnp.float32) * 2.0) / HD)
    extended = positions[0] + jnp.arange(-WINDOW, local, dtype=jnp.int32)
    angle = extended.astype(jnp.float32)[:, None] * freq[None, :]
    cosine, sine = jnp.cos(angle), jnp.sin(angle)
    query, key = normed_part(
        prep_kernel,
        (
            jax.ShapeDtypeStruct(queries.shape, jnp.bfloat16),
            jax.ShapeDtypeStruct(keys.shape, jnp.bfloat16),
        ),
        queries, keys, q_gain, k_gain, cosine, sine,
    )
    slab, query, before = lax.optimization_barrier((slab, query, before))

    rows, wide = slab.shape
    parts = slab.reshape(NZ, rows // NZ, NH, wide // NH).transpose(0, 2, 1, 3)
    parts = parts.reshape(NZ * NH, rows // NZ, wide // NH)
    parts = lax.all_to_all(parts, ("z", "head"), split_axis=0, concat_axis=0, tiled=True)
    (key_before,) = normed_part(
        halo_kernel,
        (jax.ShapeDtypeStruct((WINDOW, keys.shape[1]), jnp.bfloat16),),
        before, k_gain, cosine, sine,
    )

    def band(part, first):
        return band_part(part, 3, first, query, key, values, key_before, before)

    states = [band(0, first)]
    parts, top = lax.optimization_barrier((parts, states[0][0]))
    states[0] = (top, *states[0][1:])
    mine = pick(parts.reshape(NZ, NH, rows // NZ, wide // NH), root_z)
    mine = mine.reshape(NH * rows // NZ, wide // NH)
    mine, first = lax.optimization_barrier((mine, first))

    across = round_z(mine, NZ // 2)
    states.append(band(1, first))
    across, top = lax.optimization_barrier((across, states[1][0]))
    states[1] = (top, *states[1][1:])
    mine = jnp.concatenate([mine, across], axis=0)
    mine, first = lax.optimization_barrier((mine, first))

    around = [round_z(mine, 1), round_z(mine, -1), round_z(mine, 2)]
    far = swapped(mine, "yh")
    states.append(band(2, first))
    around, far, top = lax.optimization_barrier((around, far, states[2][0]))
    states[2] = (top, *states[2][1:])

    far_around = swapped(jnp.concatenate(around, axis=0), "yh")
    mine = jnp.concatenate([mine, *around], axis=0)
    state = prefix_part(
        False, query, states, mine, swapped(mine, "core"), far, swapped(far, "core")
    )
    far_around, top = lax.optimization_barrier((far_around, state[0]))
    last = swapped(far_around, "core")
    state = prefix_part(False, query, [(top, *state[1:])], far_around)
    return prefix_part(True, query, [state], last)


def solution(mesh):
    fine = Mesh(mesh.devices.reshape(YH, NZ, NC, NH), SEQ + ("head",))
    return jax.shard_map(
        on_device,
        mesh=fine,
        in_specs=(
            P(SEQ, "head"),
            P(SEQ, "head"),
            P(SEQ, "head"),
            P(),
            P(),
            P(SEQ),
            P(SEQ, "head", None),
            P(),
        ),
        out_specs=P(SEQ, "head"),
        check_vma=False,
    )
```

```python
import functools

import jax
import jax.numpy as jnp
from jax import lax
from jax.experimental import pallas as pl
from jax.experimental.pallas import tpu as pltpu
from jax.sharding import Mesh, PartitionSpec as P

HD = 128
WINDOW = 1024
QSCALAR = 168
YH, NZ, NC, NH = 2, 8, 2, 8
SEQ = ("yh", "z", "core")
BAND_TILE = 256
TILE = 512
CHUNK = 256
NEG = -1e30
BIG = 1e30
VMEM_LIMIT = 24 * 1024 * 1024


def swapped(array, axis):
    return lax.ppermute(array, axis, [(0, 1), (1, 0)])


def round_z(array, r):
    return lax.ppermute(array, "z", [(i, (i + r) % NZ) for i in range(NZ)])


def pick(array, at):
    return lax.dynamic_index_in_dim(array, at, 0, keepdims=False)


def halved(part, axis, root_at):
    at = lax.axis_index(axis)
    part = part.reshape(2, part.shape[0] // 2, part.shape[1])
    came = swapped(pick(part, 1 - at), axis)
    return jnp.where(root_at == at, pick(part, at), came)


def tables(cos_ref, sin_ref, at, gain, scale):
    cosine, sine = cos_ref[at, :], sin_ref[at, :]
    cosine = jnp.concatenate([cosine, cosine], axis=1)
    sine = jnp.concatenate([-sine, sine], axis=1)
    return cosine * (gain * scale), sine * (pltpu.roll(gain, HD // 2, 1) * scale)


def normed(rows, direct, crossed):
    wide = rows.astype(jnp.float32)
    square = wide * wide
    high = square.astype(jnp.bfloat16)
    low = (square - high.astype(jnp.float32)).astype(jnp.bfloat16)
    even = jnp.full((HD, HD), 1.0 / HD, jnp.bfloat16)
    mean_sq = jnp.dot(high, even, preferred_element_type=jnp.float32)
    mean_sq = mean_sq + jnp.dot(low, even, preferred_element_type=jnp.float32)
    other = pltpu.roll(rows, HD // 2, 1).astype(jnp.float32)
    return ((wide * direct + other * crossed) * lax.rsqrt(mean_sq + 1e-06)).astype(jnp.bfloat16)


def dot_t(a, b):
    return lax.dot_general(a, b, (((1,), (1,)), ((), ())), preferred_element_type=jnp.float32)


def rows_at(t, tile):
    return pl.ds(pl.multiple_of(t * tile, tile), tile)


def columns_of(h):
    return slice(h * HD, (h + 1) * HD)


def stacked(ref, at, heads):
    return jnp.concatenate([ref[at, columns_of(h)] for h in heads], axis=0)


def prep_kernel(q_ref, k_ref, qg_ref, kg_ref, cos_ref, sin_ref, qn_ref, kn_ref):
    def own(t, _):
        at = rows_at(t, BAND_TILE)
        at_table = rows_at(t + WINDOW // BAND_TILE, BAND_TILE)
        q_tables = tables(cos_ref, sin_ref, at_table, qg_ref[...], QSCALAR ** (-0.5))
        k_tables = tables(cos_ref, sin_ref, at_table, kg_ref[...], 1.0)
        for c in range(k_ref.shape[1] // HD):
            kn_ref[at, columns_of(c)] = normed(k_ref[at, columns_of(c)], *k_tables)
        for h in range(q_ref.shape[1] // HD):
            qn_ref[at, columns_of(h)] = normed(q_ref[at, columns_of(h)], *q_tables)
        return 0

    lax.fori_loop(0, q_ref.shape[0] // BAND_TILE, own, 0)


def halo_kernel(k_ref, kg_ref, cos_ref, sin_ref, kn_ref):
    def one(t, _):
        at = rows_at(t, BAND_TILE)
        k_tables = tables(cos_ref, sin_ref, at, kg_ref[...], 1.0)
        for c in range(kn_ref.shape[1] // HD):
            kn_ref[at, columns_of(c)] = normed(k_ref[at, columns_of(c)], *k_tables)
        return 0

    lax.fori_loop(0, WINDOW // BAND_TILE, one, 0)


def attend(state, query, key, value, keep_score=None, dead=None):
    score = dot_t(query, key)
    if keep_score is not None:
        score = jnp.where(keep_score, score, NEG)
    top = jnp.max(score, axis=1, keepdims=True)
    if dead is not None:
        top = jnp.where(dead, NEG, top)
    top = jnp.broadcast_to(top, query.shape)
    if state is not None:
        top = jnp.maximum(state[0], top)
    minus = top if dead is None else jnp.where(dead, BIG, top)
    weight = jnp.concatenate(
        [jnp.exp(score[:, i : i + HD] - minus).astype(jnp.bfloat16) for i in range(0, score.shape[1], HD)],
        axis=1,
    )
    value = jnp.concatenate([value, jnp.ones_like(value)], axis=1)
    out = jnp.dot(weight, value, preferred_element_type=jnp.float32)
    summed, total = out[:, :HD], out[:, HD:]
    if state is not None:
        keep = jnp.exp(state[0] - top)
        summed, total = state[1] * keep + summed, state[2] * keep + total
    return top, summed, total


def band_kernel(part, halo_rows, first_ref, q_ref, k_ref, v_ref, *rest):
    kb_ref, vb_ref = rest[:2] if halo_rows else (None, None)
    outs = rest[-3:]
    kv = k_ref.shape[1] // HD
    group = q_ref.shape[1] // HD // kv
    rows_in = lax.broadcasted_iota(jnp.int32, (group * BAND_TILE, CHUNK), 0) % BAND_TILE
    columns_in = lax.broadcasted_iota(jnp.int32, (group * BAND_TILE, CHUNK), 1)
    early = columns_in > rows_in
    late = columns_in <= rows_in
    reach = WINDOW // CHUNK
    is_first = first_ref[0] == 1
    tiles = q_ref.shape[0] // BAND_TILE
    for t in range(tiles):
        at = slice(t * BAND_TILE, (t + 1) * BAND_TILE)
        queries = [stacked(q_ref, at, range(c * group, (c + 1) * group)) for c in range(kv)]
        state = [None] * kv
        for j in range(reach, -1, -1):
            e = part * tiles + t + j - reach
            mine = e >= 0
            start = e * CHUNK if mine else halo_rows + e * CHUNK
            keys_at = slice(start, start + CHUNK)
            for c in range(kv):
                state[c] = attend(
                    state[c],
                    queries[c],
                    (k_ref if mine else kb_ref)[keys_at, columns_of(c)],
                    (v_ref if mine else vb_ref)[keys_at, columns_of(c)],
                    keep_score=late if j == reach else early if j == 0 else None,
                    dead=None if mine else is_first,
                )
        for c in range(kv):
            for g in range(group):
                rows = slice(g * BAND_TILE, (g + 1) * BAND_TILE)
                for ref, value in zip(outs, state[c]):
                    ref[at, columns_of(c * group + g)] = value[rows]


def blocks_of(p_refs):
    blocks, held, room = [], [], CHUNK
    for p_ref in p_refs:
        start = 0
        while start < p_ref.shape[0]:
            rows = min(room, p_ref.shape[0] - start)
            held.append((p_ref, start, rows))
            start, room = start + rows, room - rows
            if room == 0:
                blocks.append(held)
                held, room = [], CHUNK
    if held and blocks and CHUNK - room < CHUNK:
        blocks[-1] = blocks[-1] + held
    elif held:
        blocks.append(held)
    return blocks


def joined(block, h):
    parts = [p_ref[start : start + rows, columns_of(h)] for p_ref, start, rows in block]
    return parts[0] if len(parts) == 1 else jnp.concatenate(parts, axis=0)


def prefix_kernel(last, bands, pieces, q_ref, *rest):
    states, rest = [rest[3 * i : 3 * i + 3] for i in range(bands)], rest[3 * bands :]
    p_refs, outs = rest[:pieces], rest[pieces:]
    kv = p_refs[0].shape[1] // (2 * HD)
    group = q_ref.shape[1] // HD // kv
    each = states[0][0].shape[0]

    def step(t, state_refs, at_in):
        at = rows_at(t, TILE)
        heads = [range(c * group, (c + 1) * group) for c in range(kv)]
        queries = [stacked(q_ref, at, heads[c]) for c in range(kv)]
        state = [tuple(stacked(ref, at_in, heads[c]) for ref in state_refs) for c in range(kv)]
        for block in blocks_of(p_refs):
            for c in range(kv):
                state[c] = attend(state[c], queries[c], joined(block, 2 * c), joined(block, 2 * c + 1))
        for c in range(kv):
            result = [(state[c][1] / state[c][2]).astype(jnp.bfloat16)] if last else state[c]
            for g in range(group):
                rows = slice(g * TILE, (g + 1) * TILE)
                for ref, part in zip(outs, result):
                    ref[at, columns_of(c * group + g)] = part[rows]

    if bands > 1:
        for i in range(q_ref.shape[0] // TILE):
            step(i, states[i * TILE // each], slice(i * TILE % each, i * TILE % each + TILE))
    else:

        def one(t, _):
            step(t, states[0], rows_at(t, TILE))
            return 0

        lax.fori_loop(0, q_ref.shape[0] // TILE, one, 0)


WHOLE = pl.BlockSpec(memory_space=pltpu.VMEM)
PARAMS = pltpu.CompilerParams(vmem_limit_bytes=VMEM_LIMIT)


def cost(pairs, in_out):
    return pl.CostEstimate(flops=8 * pairs * HD, transcendentals=pairs, bytes_accessed=in_out)


def normed_part(kernel, outs, *args):
    size = sum(o.size for o in outs)
    return pl.pallas_call(
        kernel,
        out_shape=outs,
        in_specs=[WHOLE] * len(args),
        out_specs=(WHOLE,) * len(outs),
        compiler_params=PARAMS,
        cost_estimate=pl.CostEstimate(flops=60 * size, transcendentals=size // HD, bytes_accessed=6 * size),
        name="norm_rope",
    )(*args)


def band_part(part, parts, first, q, k, v, key_before, before):
    width, wide = q.shape[1], k.shape[1]
    rows = q.shape[0] // parts
    halo_rows = max(0, WINDOW - part * rows)
    own = pl.BlockSpec(((part + 1) * rows, wide), lambda i: (0, 0))
    operands = [first, q, k, v]
    in_specs = [
        pl.BlockSpec(memory_space=pltpu.SMEM),
        pl.BlockSpec((rows, width), lambda i: (part, 0)),
        own,
        own,
    ]
    if halo_rows:
        at = WINDOW // halo_rows - 1
        operands += [key_before, before]
        in_specs += [
            pl.BlockSpec((halo_rows, wide), lambda i: (at, 0)),
            pl.BlockSpec((halo_rows, wide), lambda i: (at, 1)),
        ]
    return pl.pallas_call(
        functools.partial(band_kernel, part, halo_rows),
        grid=(1,),
        out_shape=(jax.ShapeDtypeStruct((rows, width), jnp.float32),) * 3,
        in_specs=in_specs,
        out_specs=(WHOLE,) * 3,
        compiler_params=PARAMS,
        cost_estimate=cost(rows * (width // HD) * (WINDOW + BAND_TILE), 5 << 20),
        name="band",
    )(*operands)


def prefix_part(last, q, states, *pieces):
    local, width = q.shape
    flat = [part for state in states for part in state]
    if last:
        out_shape = jax.ShapeDtypeStruct((local, width), jnp.bfloat16)
        out_specs = WHOLE
    else:
        out_shape = (jax.ShapeDtypeStruct((local, width), jnp.float32),) * 3
        out_specs = (WHOLE,) * 3
    return pl.pallas_call(
        functools.partial(prefix_kernel, last, len(states), len(pieces)),
        out_shape=out_shape,
        in_specs=[WHOLE] * (1 + len(flat) + len(pieces)),
        out_specs=out_specs,
        compiler_params=PARAMS,
        cost_estimate=cost(local * (width // HD) * sum(p.shape[0] for p in pieces), 10 << 20),
        name="prefix_last" if last else "prefix",
    )(q, *flat, *pieces)


def on_device(queries, keys, values, q_gain, k_gain, positions, prefix_cache, owner):
    local = queries.shape[0]
    root = owner[0]
    root_y, root_z, root_c = root // (NZ * NC), (root // NC) % NZ, root % NC
    q_gain, k_gain = (1.0 + q_gain)[None], (1.0 + k_gain)[None]
    first = (lax.axis_index(SEQ) == 0).astype(jnp.int32).reshape(1)

    slab = halved(prefix_cache[0], "core", root_c)
    onward = [(i, i + 1) for i in range(YH * NZ * NC - 1)]
    tail = jnp.concatenate([keys[local - WINDOW :], values[local - WINDOW :]], axis=1)
    slab, tail = lax.optimization_barrier((slab, tail))
    before = lax.ppermute(tail, SEQ, onward)
    slab = halved(slab, "yh", root_y)

    half = HD // 2
    freq = 10000.0 ** (-(jnp.arange(half).astype(jnp.float32) * 2.0) / HD)
    extended = positions[0] + jnp.arange(-WINDOW, local, dtype=jnp.int32)
    angle = extended.astype(jnp.float32)[:, None] * freq[None, :]
    cosine, sine = jnp.cos(angle), jnp.sin(angle)
    query, key = normed_part(
        prep_kernel,
        (
            jax.ShapeDtypeStruct(queries.shape, jnp.bfloat16),
            jax.ShapeDtypeStruct(keys.shape, jnp.bfloat16),
        ),
        queries, keys, q_gain, k_gain, cosine, sine,
    )
    slab, query, before = lax.optimization_barrier((slab, query, before))

    rows, wide = slab.shape
    parts = slab.reshape(NZ, rows // NZ, NH, wide // NH).transpose(0, 2, 1, 3)
    parts = parts.reshape(NZ * NH, rows // NZ, wide // NH)
    parts = lax.all_to_all(parts, ("z", "head"), split_axis=0, concat_axis=0, tiled=True)
    (key_before,) = normed_part(
        halo_kernel,
        (jax.ShapeDtypeStruct((WINDOW, keys.shape[1]), jnp.bfloat16),),
        before, k_gain, cosine, sine,
    )

    def band(part, first):
        return band_part(part, 3, first, query, key, values, key_before, before)

    states = [band(0, first)]
    parts, top = lax.optimization_barrier((parts, states[0][0]))
    states[0] = (top, *states[0][1:])
    mine = pick(parts.reshape(NZ, NH, rows // NZ, wide // NH), root_z)
    mine = mine.reshape(NH * rows // NZ, wide // NH)
    mine, first = lax.optimization_barrier((mine, first))

    far = swapped(mine, "yh")
    states.append(band(1, first))
    far, top = lax.optimization_barrier((far, states[1][0]))
    states[1] = (top, *states[1][1:])
    pair = jnp.concatenate([mine, far], axis=0)
    pair, first = lax.optimization_barrier((pair, first))

    second = [round_z(pair, NZ // 2), round_z(pair, 2), round_z(pair, -2)]
    states.append(band(2, first))
    second, top = lax.optimization_barrier((second, states[2][0]))
    states[2] = (top, *states[2][1:])
    near = jnp.concatenate([pair, *second], axis=0)
    near_sibling = swapped(near, "core")
    double = jnp.concatenate([pair, second[0]], axis=0)
    third = [round_z(double, 1), round_z(double, -1)]
    state = prefix_part(False, query, states, near, near_sibling)
    third, top = lax.optimization_barrier((third, state[0]))
    third = jnp.concatenate(third, axis=0)
    third_sibling = swapped(third, "core")
    state = prefix_part(False, query, [(top, *state[1:])], third)
    return prefix_part(True, query, [state], third_sibling)


def solution(mesh):
    fine = Mesh(mesh.devices.reshape(YH, NZ, NC, NH), SEQ + ("head",))
    return jax.shard_map(
        on_device,
        mesh=fine,
        in_specs=(
            P(SEQ, "head"),
            P(SEQ, "head"),
            P(SEQ, "head"),
            P(),
            P(),
            P(SEQ),
            P(SEQ, "head", None),
            P(),
        ),
        out_specs=P(SEQ, "head"),
        check_vma=False,
    )
```

```python
import functools

import jax
import jax.numpy as jnp
from jax import lax
from jax.experimental import pallas as pl
from jax.experimental.pallas import tpu as pltpu
from jax.sharding import Mesh, PartitionSpec as P

HD = 128
WINDOW = 1024
QSCALAR = 168
YH, NZ, NC, NH = 2, 8, 2, 8
SEQ = ("yh", "z", "core")
BAND_TILE = 256
TILE = 512
CHUNK = 256
NEG = -1e30
BIG = 1e30
VMEM_LIMIT = 24 * 1024 * 1024


def swapped(array, axis):
    return lax.ppermute(array, axis, [(0, 1), (1, 0)])


def round_z(array, r):
    return lax.ppermute(array, "z", [(i, (i + r) % NZ) for i in range(NZ)])


def pick(array, at):
    return lax.dynamic_index_in_dim(array, at, 0, keepdims=False)


def owner_at(owner_ref):
    root = owner_ref[0]
    return root // (NZ * NC), (root // NC) % NZ, root % NC


def copied(source, target, sems):
    rows = target.shape[0] // sems.shape[0]
    copies = [
        pltpu.make_async_copy(
            source.at[pl.ds(i * rows, rows)], target.at[pl.ds(i * rows, rows)], sems.at[i]
        )
        for i in range(sems.shape[0])
    ]
    for copy in copies:
        copy.start()
    for copy in copies:
        copy.wait()


def other_half_kernel(slab_ref, out_ref, sems):
    rows = out_ref.shape[0]
    copied(slab_ref.at[pl.ds((1 - lax.axis_index("core")) * rows, rows)], out_ref, sems)


def quarter_of(owner_ref, slab_ref, sibling_ref, of_y, out_ref, sems):
    core, rows = lax.axis_index("core"), out_ref.shape[0]
    mine = owner_at(owner_ref)[2] == core

    @pl.when(mine)
    def _():
        copied(slab_ref.at[pl.ds((core * YH + of_y) * rows, rows)], out_ref, sems)

    @pl.when(jnp.logical_not(mine))
    def _():
        copied(sibling_ref.at[pl.ds(of_y * rows, rows)], out_ref, sems)


def far_quarter_kernel(owner_ref, slab_ref, sibling_ref, out_ref, sems):
    quarter_of(owner_ref, slab_ref, sibling_ref, 1 - lax.axis_index("yh"), out_ref, sems)


def own_quarter_kernel(owner_ref, slab_ref, sibling_ref, came_ref, out_ref, sems):
    y = lax.axis_index("yh")
    mine = owner_at(owner_ref)[0] == y

    @pl.when(mine)
    def _():
        quarter_of(owner_ref, slab_ref, sibling_ref, y, out_ref, sems)

    @pl.when(jnp.logical_not(mine))
    def _():
        copied(came_ref, out_ref, sems)


def moved(kernel, rows, *operands):
    specs = [
        pl.BlockSpec(memory_space=pltpu.SMEM if o.dtype == jnp.int32 else pl.ANY) for o in operands
    ]
    return pl.pallas_call(
        kernel,
        out_shape=jax.ShapeDtypeStruct((rows, operands[-1].shape[1]), jnp.bfloat16),
        in_specs=specs,
        out_specs=pl.BlockSpec(memory_space=pl.ANY),
        scratch_shapes=[pltpu.SemaphoreType.DMA((4,))],
        name="slab_rows",
    )(*operands)


def tables(cos_ref, sin_ref, at, gain, scale):
    cosine, sine = cos_ref[at, :], sin_ref[at, :]
    cosine = jnp.concatenate([cosine, cosine], axis=1)
    sine = jnp.concatenate([-sine, sine], axis=1)
    return cosine * (gain * scale), sine * (pltpu.roll(gain, HD // 2, 1) * scale)


def normed(rows, direct, crossed):
    wide = rows.astype(jnp.float32)
    square = wide * wide
    high = square.astype(jnp.bfloat16)
    low = (square - high.astype(jnp.float32)).astype(jnp.bfloat16)
    even = jnp.full((HD, HD), 1.0 / HD, jnp.bfloat16)
    mean_sq = jnp.dot(high, even, preferred_element_type=jnp.float32)
    mean_sq = mean_sq + jnp.dot(low, even, preferred_element_type=jnp.float32)
    other = pltpu.roll(rows, HD // 2, 1).astype(jnp.float32)
    return ((wide * direct + other * crossed) * lax.rsqrt(mean_sq + 1e-06)).astype(jnp.bfloat16)


def dot_t(a, b):
    return lax.dot_general(a, b, (((1,), (1,)), ((), ())), preferred_element_type=jnp.float32)


def rows_at(t, tile):
    return pl.ds(pl.multiple_of(t * tile, tile), tile)


def columns_of(h):
    return slice(h * HD, (h + 1) * HD)


def stacked(ref, at, heads):
    return jnp.concatenate([ref[at, columns_of(h)] for h in heads], axis=0)


def prep_kernel(
    q_ref, k_ref, qg_ref, kg_ref, cos_ref, sin_ref, qn_ref, kn_ref, qi_ref, ki_ref, qs_ref, ks_ref, in_sems, out_sems
):
    tiles = q_ref.shape[0] // BAND_TILE

    def copies(t, pairs, sems):
        at = rows_at(t, BAND_TILE)
        return [
            pltpu.make_async_copy(source.at[at], target.at[at], sems.at[i, t])
            for i, (source, target) in enumerate(pairs)
        ]

    into = ((q_ref, qi_ref), (k_ref, ki_ref))
    out = ((qs_ref, qn_ref), (ks_ref, kn_ref))
    for t in range(tiles):
        for copy in copies(t, into, in_sems):
            copy.start()

    def own(t, _):
        at = rows_at(t, BAND_TILE)
        at_table = rows_at(t + WINDOW // BAND_TILE, BAND_TILE)
        q_tables = tables(cos_ref, sin_ref, at_table, qg_ref[...], QSCALAR ** (-0.5))
        k_tables = tables(cos_ref, sin_ref, at_table, kg_ref[...], 1.0)
        for copy in copies(t, into, in_sems):
            copy.wait()
        for c in range(k_ref.shape[1] // HD):
            ks_ref[at, columns_of(c)] = normed(ki_ref[at, columns_of(c)], *k_tables)
        for h in range(q_ref.shape[1] // HD):
            qs_ref[at, columns_of(h)] = normed(qi_ref[at, columns_of(h)], *q_tables)
        for copy in copies(t, out, out_sems):
            copy.start()
        return 0

    lax.fori_loop(0, tiles, own, 0)
    for t in range(tiles):
        for copy in copies(t, out, out_sems):
            copy.wait()


def halo_kernel(k_ref, kg_ref, cos_ref, sin_ref, kn_ref):
    def one(t, _):
        at = rows_at(t, BAND_TILE)
        k_tables = tables(cos_ref, sin_ref, at, kg_ref[...], 1.0)
        for c in range(kn_ref.shape[1] // HD):
            kn_ref[at, columns_of(c)] = normed(k_ref[at, columns_of(c)], *k_tables)
        return 0

    lax.fori_loop(0, WINDOW // BAND_TILE, one, 0)


def attend(state, query, key, value, keep_score=None, dead=None):
    score = dot_t(query, key)
    if keep_score is not None:
        score = jnp.where(keep_score, score, NEG)
    top = jnp.max(score, axis=1, keepdims=True)
    if dead is not None:
        top = jnp.where(dead, NEG, top)
    top = jnp.broadcast_to(top, query.shape)
    if state is not None:
        top = jnp.maximum(state[0], top)
    minus = top if dead is None else jnp.where(dead, BIG, top)
    weight = jnp.concatenate(
        [jnp.exp(score[:, i : i + HD] - minus).astype(jnp.bfloat16) for i in range(0, score.shape[1], HD)],
        axis=1,
    )
    value = jnp.concatenate([value, jnp.ones_like(value)], axis=1)
    out = jnp.dot(weight, value, preferred_element_type=jnp.float32)
    summed, total = out[:, :HD], out[:, HD:]
    if state is not None:
        keep = jnp.exp(state[0] - top)
        summed, total = state[1] * keep + summed, state[2] * keep + total
    return top, summed, total


def band_kernel(part, halo_rows, to_hbm, first_ref, *rest):
    count = 5 if halo_rows else 3
    sources, outs, rest = rest[:count], rest[count : count + 3], rest[count + 3 :]
    held, in_sems, rest = rest[:count], rest[count], rest[count + 1 :]
    rows, kv = held[0].shape[0], held[1].shape[1] // HD
    before_at = pl.ds(WINDOW - halo_rows, halo_rows)
    whats = [
        sources[0].at[pl.ds(part * rows, rows)],
        sources[1].at[pl.ds(0, (part + 1) * rows)],
        sources[2].at[pl.ds(0, (part + 1) * rows)],
    ]
    if halo_rows:
        whats += [sources[3].at[before_at], sources[4].at[before_at, pl.ds(kv * HD, kv * HD)]]
    copies = [
        pltpu.make_async_copy(what, where, in_sems.at[i])
        for i, (what, where) in enumerate(zip(whats, held))
    ]
    for copy in copies:
        copy.start()
    for copy in copies:
        copy.wait()
    q_ref, k_ref, v_ref = held[:3]
    kb_ref, vb_ref = held[3:] if halo_rows else (None, None)
    stores, out_sems = (rest[:3], rest[3]) if to_hbm else (outs, None)

    group = q_ref.shape[1] // HD // kv
    rows_in = lax.broadcasted_iota(jnp.int32, (group * BAND_TILE, CHUNK), 0) % BAND_TILE
    columns_in = lax.broadcasted_iota(jnp.int32, (group * BAND_TILE, CHUNK), 1)
    early = columns_in > rows_in
    late = columns_in <= rows_in
    reach = WINDOW // CHUNK
    is_first = first_ref[0] == 1
    tiles = rows // BAND_TILE
    sent = []
    for t in range(tiles):
        at = slice(t * BAND_TILE, (t + 1) * BAND_TILE)
        queries = [stacked(q_ref, at, range(c * group, (c + 1) * group)) for c in range(kv)]
        state = [None] * kv
        for j in range(reach, -1, -1):
            e = part * tiles + t + j - reach
            mine = e >= 0
            start = e * CHUNK if mine else halo_rows + e * CHUNK
            keys_at = slice(start, start + CHUNK)
            for c in range(kv):
                state[c] = attend(
                    state[c],
                    queries[c],
                    (k_ref if mine else kb_ref)[keys_at, columns_of(c)],
                    (v_ref if mine else vb_ref)[keys_at, columns_of(c)],
                    keep_score=late if j == reach else early if j == 0 else None,
                    dead=None if mine else is_first,
                )
        for c in range(kv):
            for g in range(group):
                of_head = slice(g * BAND_TILE, (g + 1) * BAND_TILE)
                for ref, value in zip(stores, state[c]):
                    ref[at, columns_of(c * group + g)] = value[of_head]
        if to_hbm:
            at_rows = pl.ds(t * BAND_TILE, BAND_TILE)
            for i in range(3):
                copy = pltpu.make_async_copy(stores[i].at[at_rows], outs[i].at[at_rows], out_sems.at[i, t])
                copy.start()
                sent.append(copy)
    for copy in sent:
        copy.wait()


def blocks_of(p_refs):
    blocks, held, room = [], [], CHUNK
    for p_ref in p_refs:
        start = 0
        while start < p_ref.shape[0]:
            rows = min(room, p_ref.shape[0] - start)
            held.append((p_ref, start, rows))
            start, room = start + rows, room - rows
            if room == 0:
                blocks.append(held)
                held, room = [], CHUNK
    if held and blocks and CHUNK - room < CHUNK:
        blocks[-1] = blocks[-1] + held
    elif held:
        blocks.append(held)
    return blocks


def joined(block, h):
    parts = [p_ref[start : start + rows, columns_of(h)] for p_ref, start, rows in block]
    return parts[0] if len(parts) == 1 else jnp.concatenate(parts, axis=0)


def prefix_kernel(last, bands, pieces, q_ref, *rest):
    states, rest = [rest[3 * i : 3 * i + 3] for i in range(bands)], rest[3 * bands :]
    p_refs, outs = rest[:pieces], rest[pieces:]
    if last:
        out_ref, store_ref, sems = outs
        outs = (store_ref,)
        sent = [
            pltpu.make_async_copy(store_ref.at[rows_at(t, TILE)], out_ref.at[rows_at(t, TILE)], sems.at[t])
            for t in range(q_ref.shape[0] // TILE)
        ]
    kv = p_refs[0].shape[1] // (2 * HD)
    group = q_ref.shape[1] // HD // kv
    each = states[0][0].shape[0]

    def step(t, state_refs, at_in):
        at = rows_at(t, TILE)
        heads = [range(c * group, (c + 1) * group) for c in range(kv)]
        queries = [stacked(q_ref, at, heads[c]) for c in range(kv)]
        state = [tuple(stacked(ref, at_in, heads[c]) for ref in state_refs) for c in range(kv)]
        for block in blocks_of(p_refs):
            for c in range(kv):
                state[c] = attend(state[c], queries[c], joined(block, 2 * c), joined(block, 2 * c + 1))
        for c in range(kv):
            result = [(state[c][1] / state[c][2]).astype(jnp.bfloat16)] if last else state[c]
            for g in range(group):
                rows = slice(g * TILE, (g + 1) * TILE)
                for ref, part in zip(outs, result):
                    ref[at, columns_of(c * group + g)] = part[rows]

    if bands > 1:
        for i in range(q_ref.shape[0] // TILE):
            step(i, states[i * TILE // each], slice(i * TILE % each, i * TILE % each + TILE))
    elif last:
        for t in range(q_ref.shape[0] // TILE):
            step(t, states[0], slice(t * TILE, (t + 1) * TILE))
            sent[t].start()
        for copy in sent:
            copy.wait()
    else:

        def one(t, _):
            step(t, states[0], rows_at(t, TILE))
            return 0

        lax.fori_loop(0, q_ref.shape[0] // TILE, one, 0)


WHOLE = pl.BlockSpec(memory_space=pltpu.VMEM)
ALONE = pltpu.CompilerParams(vmem_limit_bytes=60 * 1024 * 1024)
IN_HBM = pl.BlockSpec(memory_space=pltpu.HBM)
PARAMS = pltpu.CompilerParams(vmem_limit_bytes=VMEM_LIMIT)


def cost(pairs, in_out):
    return pl.CostEstimate(flops=8 * pairs * HD, transcendentals=pairs, bytes_accessed=in_out)


def prep(*args):
    q, k = args[:2]
    tiles = q.shape[0] // BAND_TILE
    return pl.pallas_call(
        prep_kernel,
        out_shape=tuple(jax.ShapeDtypeStruct(a.shape, jnp.bfloat16) for a in (q, k)),
        in_specs=[IN_HBM] * 2 + [WHOLE] * 4,
        out_specs=(IN_HBM,) * 2,
        scratch_shapes=[pltpu.VMEM(a.shape, jnp.bfloat16) for a in (q, k, q, k)]
        + [pltpu.SemaphoreType.DMA((2, tiles))] * 2,
        compiler_params=ALONE,
        cost_estimate=pl.CostEstimate(flops=q.size, transcendentals=0, bytes_accessed=q.size),
        name="norm_rope",
    )(*args)


def halo_keys(before, *args):
    return pl.pallas_call(
        halo_kernel,
        out_shape=jax.ShapeDtypeStruct((WINDOW, before.shape[1] // 2), jnp.bfloat16),
        in_specs=[WHOLE] * 4,
        out_specs=WHOLE,
        compiler_params=PARAMS,
        cost_estimate=pl.CostEstimate(flops=30 * before.size, transcendentals=0, bytes_accessed=4 * before.size),
        name="norm_rope_halo",
    )(before, *args)


def band_part(part, parts, first, q, k, v, key_before, before):
    width, wide = q.shape[1], k.shape[1]
    rows = q.shape[0] // parts
    halo_rows = max(0, WINDOW - part * rows)
    operands = [q, k, v] + ([key_before, before] if halo_rows else [])
    shapes = [(rows, width)] + [((part + 1) * rows, wide)] * 2 + ([(halo_rows, wide)] * 2 if halo_rows else [])
    scratch = [pltpu.VMEM(shape, jnp.bfloat16) for shape in shapes]
    scratch.append(pltpu.SemaphoreType.DMA((len(shapes),)))
    to_hbm = part < parts - 1
    if to_hbm:
        scratch += [pltpu.VMEM((rows, width), jnp.float32)] * 3
        scratch.append(pltpu.SemaphoreType.DMA((3, rows // BAND_TILE)))
    return pl.pallas_call(
        functools.partial(band_kernel, part, halo_rows, to_hbm),
        out_shape=(jax.ShapeDtypeStruct((rows, width), jnp.float32),) * 3,
        in_specs=[pl.BlockSpec(memory_space=pltpu.SMEM)] + [IN_HBM] * len(operands),
        out_specs=(IN_HBM if to_hbm else WHOLE,) * 3,
        scratch_shapes=scratch,
        compiler_params=ALONE if to_hbm else PARAMS,
        cost_estimate=cost(rows * (width // HD) * (WINDOW + BAND_TILE), 5 << 20),
        name="band",
    )(first, *operands)


def prefix_part(last, q, states, *pieces):
    local, width = q.shape
    flat = [part for state in states for part in state]
    scratch = []
    if last:
        out_shape = jax.ShapeDtypeStruct((local, width), jnp.bfloat16)
        out_specs = IN_HBM
        scratch = [pltpu.VMEM((local, width), jnp.bfloat16), pltpu.SemaphoreType.DMA((local // TILE,))]
    else:
        out_shape = (jax.ShapeDtypeStruct((local, width), jnp.float32),) * 3
        out_specs = (WHOLE,) * 3
    return pl.pallas_call(
        functools.partial(prefix_kernel, last, len(states), len(pieces)),
        out_shape=out_shape,
        in_specs=[WHOLE] * (1 + len(flat) + len(pieces)),
        out_specs=out_specs,
        scratch_shapes=scratch,
        compiler_params=PARAMS,
        cost_estimate=cost(local * (width // HD) * sum(p.shape[0] for p in pieces), 10 << 20),
        name="prefix_last" if last else "prefix",
    )(q, *flat, *pieces)


def on_device(queries, keys, values, q_gain, k_gain, positions, prefix_cache, owner):
    local = queries.shape[0]
    root = owner[0]
    root_z = (root // NC) % NZ
    q_gain, k_gain = (1.0 + q_gain)[None], (1.0 + k_gain)[None]
    first = (lax.axis_index(SEQ) == 0).astype(jnp.int32).reshape(1)

    whole = prefix_cache[0]
    half_rows = whole.shape[0] // NC
    sibling = swapped(moved(other_half_kernel, half_rows, whole), "core")
    onward = [(i, i + 1) for i in range(YH * NZ * NC - 1)]
    tail = jnp.concatenate([keys[local - WINDOW :], values[local - WINDOW :]], axis=1)
    sent = moved(far_quarter_kernel, half_rows // YH, owner, whole, sibling)
    sent, tail = lax.optimization_barrier((sent, tail))
    before = lax.ppermute(tail, SEQ, onward)
    came = swapped(sent, "yh")
    slab = moved(own_quarter_kernel, half_rows // YH, owner, whole, sibling, came)

    half = HD // 2
    freq = 10000.0 ** (-(jnp.arange(half).astype(jnp.float32) * 2.0) / HD)
    extended = positions[0] + jnp.arange(-WINDOW, local, dtype=jnp.int32)
    angle = extended.astype(jnp.float32)[:, None] * freq[None, :]
    cosine, sine = jnp.cos(angle), jnp.sin(angle)
    query, key = prep(queries, keys, q_gain, k_gain, cosine, sine)
    slab, query, before = lax.optimization_barrier((slab, query, before))

    rows, wide = slab.shape
    parts = slab.reshape(NZ, rows // NZ, NH, wide // NH).transpose(0, 2, 1, 3)
    parts = parts.reshape(NZ * NH, rows // NZ, wide // NH)
    parts = lax.all_to_all(parts, ("z", "head"), split_axis=0, concat_axis=0, tiled=True)
    key_before = halo_keys(before, k_gain, cosine, sine)

    def band(part, first):
        return band_part(part, 3, first, query, key, values, key_before, before)

    states = [band(0, first)]
    parts, top = lax.optimization_barrier((parts, states[0][0]))
    states[0] = (top, *states[0][1:])
    mine = pick(parts.reshape(NZ, NH, rows // NZ, wide // NH), root_z)
    mine = mine.reshape(NH * rows // NZ, wide // NH)
    mine, first = lax.optimization_barrier((mine, first))

    far = swapped(mine, "yh")
    states.append(band(1, first))
    far, top = lax.optimization_barrier((far, states[1][0]))
    states[1] = (top, *states[1][1:])
    pair = jnp.concatenate([mine, far], axis=0)
    pair, first = lax.optimization_barrier((pair, first))

    second = [round_z(pair, NZ // 2), round_z(pair, 2), round_z(pair, -2)]
    states.append(band(2, first))
    second, top = lax.optimization_barrier((second, states[2][0]))
    states[2] = (top, *states[2][1:])
    near = jnp.concatenate([pair, *second], axis=0)
    near_sibling = swapped(near, "core")
    double = jnp.concatenate([pair, second[0]], axis=0)
    third = [round_z(double, 1), round_z(double, -1)]
    state = prefix_part(False, query, states, near, near_sibling)
    third, top = lax.optimization_barrier((third, state[0]))
    third = jnp.concatenate(third, axis=0)
    third_sibling = swapped(third, "core")
    state = prefix_part(False, query, [(top, *state[1:])], third)
    return prefix_part(True, query, [state], third_sibling)


def solution(mesh):
    fine = Mesh(mesh.devices.reshape(YH, NZ, NC, NH), SEQ + ("head",))
    return jax.shard_map(
        on_device,
        mesh=fine,
        in_specs=(
            P(SEQ, "head"),
            P(SEQ, "head"),
            P(SEQ, "head"),
            P(),
            P(),
            P(SEQ),
            P(SEQ, "head", None),
            P(),
        ),
        out_specs=P(SEQ, "head"),
        check_vma=False,
    )
```

```python
import functools

import jax
import jax.numpy as jnp
from jax import lax
from jax.experimental import pallas as pl
from jax.experimental.pallas import tpu as pltpu
from jax.sharding import Mesh, PartitionSpec as P

HD = 128
WINDOW = 1024
QSCALAR = 168
YH, NZ, NC, NH = 2, 8, 2, 8
SEQ = ("yh", "z", "core")
BAND_TILE = 256
TILE = 512
CHUNK = 256
NEG = -1e30
BIG = 1e30
VMEM_LIMIT = 24 * 1024 * 1024


def swapped(array, axis):
    return lax.ppermute(array, axis, [(0, 1), (1, 0)])


def round_z(array, r):
    return lax.ppermute(array, "z", [(i, (i + r) % NZ) for i in range(NZ)])


def pick(array, at):
    return lax.dynamic_index_in_dim(array, at, 0, keepdims=False)


def owner_at(owner_ref):
    root = owner_ref[0]
    return root // (NZ * NC), (root // NC) % NZ, root % NC


def copied(source, target, sems):
    rows = target.shape[0] // sems.shape[0]
    copies = [
        pltpu.make_async_copy(
            source.at[pl.ds(i * rows, rows)], target.at[pl.ds(i * rows, rows)], sems.at[i]
        )
        for i in range(sems.shape[0])
    ]
    for copy in copies:
        copy.start()
    for copy in copies:
        copy.wait()


def other_half_kernel(slab_ref, out_ref, sems):
    rows = out_ref.shape[0]
    copied(slab_ref.at[pl.ds((1 - lax.axis_index("core")) * rows, rows)], out_ref, sems)


def quarter_of(owner_ref, slab_ref, sibling_ref, of_y, out_ref, sems):
    core, rows = lax.axis_index("core"), out_ref.shape[0]
    mine = owner_at(owner_ref)[2] == core

    @pl.when(mine)
    def _():
        copied(slab_ref.at[pl.ds((core * YH + of_y) * rows, rows)], out_ref, sems)

    @pl.when(jnp.logical_not(mine))
    def _():
        out_ref[...] = sibling_ref[rows_at(of_y, rows), :]


def far_quarter_kernel(owner_ref, slab_ref, sibling_ref, out_ref, sems):
    quarter_of(owner_ref, slab_ref, sibling_ref, 1 - lax.axis_index("yh"), out_ref, sems)


def own_quarter_kernel(owner_ref, slab_ref, sibling_ref, came_ref, out_ref, sems):
    y = lax.axis_index("yh")
    mine = owner_at(owner_ref)[0] == y

    @pl.when(mine)
    def _():
        quarter_of(owner_ref, slab_ref, sibling_ref, y, out_ref, sems)

    @pl.when(jnp.logical_not(mine))
    def _():
        out_ref[...] = came_ref[...]


def moved(kernel, rows, slab, *received, owner=None):
    front = [] if owner is None else [owner]
    return pl.pallas_call(
        kernel,
        out_shape=jax.ShapeDtypeStruct((rows, slab.shape[1]), jnp.bfloat16),
        in_specs=[pl.BlockSpec(memory_space=pltpu.SMEM)] * len(front)
        + [pl.BlockSpec(memory_space=pltpu.HBM)]
        + [pl.BlockSpec(memory_space=pltpu.VMEM)] * len(received),
        out_specs=pl.BlockSpec(memory_space=pltpu.VMEM),
        scratch_shapes=[pltpu.SemaphoreType.DMA((4,))],
        compiler_params=pltpu.CompilerParams(vmem_limit_bytes=12 * 1024 * 1024),
        name="slab_rows",
    )(*front, slab, *received)


def tables(cos_ref, sin_ref, at, gain, scale):
    cosine, sine = cos_ref[at, :], sin_ref[at, :]
    cosine = jnp.concatenate([cosine, cosine], axis=1)
    sine = jnp.concatenate([-sine, sine], axis=1)
    return cosine * (gain * scale), sine * (pltpu.roll(gain, HD // 2, 1) * scale)


def normed(rows, direct, crossed):
    wide = rows.astype(jnp.float32)
    square = wide * wide
    high = square.astype(jnp.bfloat16)
    low = (square - high.astype(jnp.float32)).astype(jnp.bfloat16)
    even = jnp.full((HD, HD), 1.0 / HD, jnp.bfloat16)
    mean_sq = jnp.dot(high, even, preferred_element_type=jnp.float32)
    mean_sq = mean_sq + jnp.dot(low, even, preferred_element_type=jnp.float32)
    other = pltpu.roll(rows, HD // 2, 1).astype(jnp.float32)
    return ((wide * direct + other * crossed) * lax.rsqrt(mean_sq + 1e-06)).astype(jnp.bfloat16)


def dot_t(a, b):
    return lax.dot_general(a, b, (((1,), (1,)), ((), ())), preferred_element_type=jnp.float32)


def rows_at(t, tile):
    return pl.ds(pl.multiple_of(t * tile, tile), tile)


def columns_of(h):
    return slice(h * HD, (h + 1) * HD)


def stacked(ref, at, heads):
    return jnp.concatenate([ref[at, columns_of(h)] for h in heads], axis=0)


def prep_kernel(q_ref, k_ref, qg_ref, kg_ref, cos_ref, sin_ref, qn_ref, kn_ref):
    def own(t, _):
        at = rows_at(t, BAND_TILE)
        at_table = rows_at(t + WINDOW // BAND_TILE, BAND_TILE)
        q_tables = tables(cos_ref, sin_ref, at_table, qg_ref[...], QSCALAR ** (-0.5))
        k_tables = tables(cos_ref, sin_ref, at_table, kg_ref[...], 1.0)
        for c in range(k_ref.shape[1] // HD):
            kn_ref[at, columns_of(c)] = normed(k_ref[at, columns_of(c)], *k_tables)
        for h in range(q_ref.shape[1] // HD):
            qn_ref[at, columns_of(h)] = normed(q_ref[at, columns_of(h)], *q_tables)
        return 0

    lax.fori_loop(0, q_ref.shape[0] // BAND_TILE, own, 0)


def halo_kernel(near_ref, far_ref, kg_ref, cos_ref, sin_ref, kn_ref):
    def one(t, _):
        at = rows_at(t, BAND_TILE)
        k_tables = tables(cos_ref, sin_ref, at, kg_ref[...], 1.0)
        for c in range(kn_ref.shape[1] // HD):
            rows = near_ref[at, columns_of(c)] + far_ref[at, columns_of(c)]
            kn_ref[at, columns_of(c)] = normed(rows, *k_tables)
        return 0

    lax.fori_loop(0, WINDOW // BAND_TILE, one, 0)


def attend(state, query, key, value, keep_score=None, dead=None):
    score = dot_t(query, key)
    if keep_score is not None:
        score = jnp.where(keep_score, score, NEG)
    top = jnp.max(score, axis=1, keepdims=True)
    if dead is not None:
        top = jnp.where(dead, NEG, top)
    top = jnp.broadcast_to(top, query.shape)
    if state is not None:
        top = jnp.maximum(state[0], top)
    minus = top if dead is None else jnp.where(dead, BIG, top)
    weight = jnp.concatenate(
        [jnp.exp(score[:, i : i + HD] - minus).astype(jnp.bfloat16) for i in range(0, score.shape[1], HD)],
        axis=1,
    )
    value = jnp.concatenate([value, jnp.ones_like(value)], axis=1)
    out = jnp.dot(weight, value, preferred_element_type=jnp.float32)
    summed, total = out[:, :HD], out[:, HD:]
    if state is not None:
        keep = jnp.exp(state[0] - top)
        summed, total = state[1] * keep + summed, state[2] * keep + total
    return top, summed, total


def triangle(group):
    rows_in = lax.broadcasted_iota(jnp.int32, (group * BAND_TILE, CHUNK), 0) % BAND_TILE
    columns_in = lax.broadcasted_iota(jnp.int32, (group * BAND_TILE, CHUNK), 1)
    return columns_in <= rows_in


def kept(refs, at, kv, group, state):
    for c in range(kv):
        for g in range(group):
            rows = slice(g * BAND_TILE, (g + 1) * BAND_TILE)
            for ref, value in zip(refs, state[c]):
                ref[at, columns_of(c * group + g)] = value[rows]


def local_kernel(from_tile, order_ref, q_ref, k_ref, v_ref, *outs):
    kv = k_ref.shape[1] // HD
    group = q_ref.shape[1] // HD // kv
    reach = WINDOW // CHUNK
    late = triangle(group)
    for t in range(q_ref.shape[0] // BAND_TILE):
        at = slice(t * BAND_TILE, (t + 1) * BAND_TILE)
        block = from_tile + t
        state = [None] * kv
        for e in range(block, max(block - reach, 0) - 1, -1):
            keys_at = slice(e * CHUNK, (e + 1) * CHUNK)
            for c in range(kv):
                state[c] = attend(
                    state[c],
                    stacked(q_ref, at, range(c * group, (c + 1) * group)),
                    k_ref[keys_at, columns_of(c)],
                    v_ref[keys_at, columns_of(c)],
                    keep_score=late if e == block else ~late if e == block - reach else None,
                )
        kept(outs, at, kv, group, state)


def before_kernel(first_ref, q_ref, k_ref, near_ref, far_ref, *rest):
    ins, outs = rest[:3], rest[3:]
    kv = k_ref.shape[1] // HD
    group = q_ref.shape[1] // HD // kv
    late = triangle(group)
    is_first = first_ref[0] == 1
    for t in range(q_ref.shape[0] // BAND_TILE):
        at = slice(t * BAND_TILE, (t + 1) * BAND_TILE)
        heads = [range(c * group, (c + 1) * group) for c in range(kv)]
        state = [tuple(stacked(ref, at, heads[c]) for ref in ins) for c in range(kv)]
        for e in range(WINDOW // CHUNK - 1, t - 1, -1):
            keys_at = slice(e * CHUNK, (e + 1) * CHUNK)
            for c in range(kv):
                state[c] = attend(
                    state[c],
                    stacked(q_ref, at, heads[c]),
                    k_ref[keys_at, columns_of(c)],
                    near_ref[keys_at, columns_of(c)] + far_ref[keys_at, columns_of(c)],
                    keep_score=~late if e == t else None,
                    dead=is_first,
                )
        kept(outs, at, kv, group, state)


def blocks_of(p_refs):
    blocks, held, room = [], [], CHUNK
    for p_ref in p_refs:
        start = 0
        while start < p_ref.shape[0]:
            rows = min(room, p_ref.shape[0] - start)
            held.append((p_ref, start, rows))
            start, room = start + rows, room - rows
            if room == 0:
                blocks.append(held)
                held, room = [], CHUNK
    if held and blocks and CHUNK - room < CHUNK:
        blocks[-1] = blocks[-1] + held
    elif held:
        blocks.append(held)
    return blocks


def joined(block, h):
    parts = [p_ref[start : start + rows, columns_of(h)] for p_ref, start, rows in block]
    return parts[0] if len(parts) == 1 else jnp.concatenate(parts, axis=0)


def prefix_kernel(last, bands, pieces, q_ref, *rest):
    states, rest = [rest[3 * i : 3 * i + 3] for i in range(bands)], rest[3 * bands :]
    p_refs, outs = rest[:pieces], rest[pieces:]
    if last:
        out_ref, store_ref, sems = outs
        outs = (store_ref,)
        sent = [
            pltpu.make_async_copy(store_ref.at[rows_at(t, TILE)], out_ref.at[rows_at(t, TILE)], sems.at[t])
            for t in range(q_ref.shape[0] // TILE)
        ]
    kv = p_refs[0].shape[1] // (2 * HD)
    group = q_ref.shape[1] // HD // kv
    state_of = [(refs, at) for refs in states for at in range(0, refs[0].shape[0], TILE)]

    def step(t, state_refs, at_in):
        at = rows_at(t, TILE)
        heads = [range(c * group, (c + 1) * group) for c in range(kv)]
        queries = [stacked(q_ref, at, heads[c]) for c in range(kv)]
        state = [tuple(stacked(ref, at_in, heads[c]) for ref in state_refs) for c in range(kv)]
        for block in blocks_of(p_refs):
            for c in range(kv):
                state[c] = attend(state[c], queries[c], joined(block, 2 * c), joined(block, 2 * c + 1))
        for c in range(kv):
            result = [(state[c][1] / state[c][2]).astype(jnp.bfloat16)] if last else state[c]
            for g in range(group):
                rows = slice(g * TILE, (g + 1) * TILE)
                for ref, part in zip(outs, result):
                    ref[at, columns_of(c * group + g)] = part[rows]

    if bands > 1:
        for i in range(q_ref.shape[0] // TILE):
            refs, start = state_of[i]
            step(i, refs, slice(start, start + TILE))
    elif last:
        for t in range(q_ref.shape[0] // TILE):
            step(t, states[0], slice(t * TILE, (t + 1) * TILE))
            sent[t].start()
        for copy in sent:
            copy.wait()
    else:

        def one(t, _):
            step(t, states[0], rows_at(t, TILE))
            return 0

        lax.fori_loop(0, q_ref.shape[0] // TILE, one, 0)


WHOLE = pl.BlockSpec(memory_space=pltpu.VMEM)
ALONE = pltpu.CompilerParams(vmem_limit_bytes=60 * 1024 * 1024)
IN_HBM = pl.BlockSpec(memory_space=pltpu.HBM)
PARAMS = pltpu.CompilerParams(vmem_limit_bytes=VMEM_LIMIT)


def cost(pairs, in_out):
    return pl.CostEstimate(flops=8 * pairs * HD, transcendentals=pairs, bytes_accessed=in_out)


def normed_part(kernel, params, outs, *args):
    size = sum(o.size for o in outs)
    return pl.pallas_call(
        kernel,
        out_shape=outs,
        in_specs=[WHOLE] * len(args),
        out_specs=(WHOLE,) * len(outs),
        compiler_params=params,
        cost_estimate=pl.CostEstimate(flops=size, transcendentals=0, bytes_accessed=size),
        name="norm_rope",
    )(*args)


def local_part(from_row, to_row, order, q, k, v, params):
    width, wide = q.shape[1], k.shape[1]
    rows = to_row - from_row
    own = pl.BlockSpec((to_row, wide), lambda i: (0, 0))
    return pl.pallas_call(
        functools.partial(local_kernel, from_row // BAND_TILE),
        grid=(1,),
        out_shape=(jax.ShapeDtypeStruct((rows, width), jnp.float32),) * 3,
        in_specs=[
            pl.BlockSpec(memory_space=pltpu.SMEM),
            pl.BlockSpec((rows, width), lambda i: (from_row // rows, 0)),
            own,
            own,
        ],
        out_specs=(WHOLE,) * 3,
        compiler_params=params,
        cost_estimate=cost(rows * (width // HD) * WINDOW, 5 << 20),
        name="band_local",
    )(order, q, k, v)


def before_part(first, q, key_before, near, far, state):
    width, wide = q.shape[1], key_before.shape[1]
    rows = state[0].shape[0]
    values = pl.BlockSpec((WINDOW, wide), lambda i: (0, 1))
    return pl.pallas_call(
        before_kernel,
        grid=(1,),
        out_shape=(jax.ShapeDtypeStruct((rows, width), jnp.float32),) * 3,
        in_specs=[
            pl.BlockSpec(memory_space=pltpu.SMEM),
            pl.BlockSpec((rows, width), lambda i: (0, 0)),
            pl.BlockSpec((WINDOW, wide), lambda i: (0, 0)),
            values,
            values,
        ]
        + [WHOLE] * 3,
        out_specs=(WHOLE,) * 3,
        compiler_params=PARAMS,
        cost_estimate=cost(rows * (width // HD) * WINDOW // 2, 5 << 20),
        name="band_before",
    )(first, q, key_before, near, far, *state)


def prefix_part(last, q, states, *pieces):
    local, width = q.shape
    flat = [part for state in states for part in state]
    scratch = []
    if last:
        out_shape = jax.ShapeDtypeStruct((local, width), jnp.bfloat16)
        out_specs = IN_HBM
        scratch = [pltpu.VMEM((local, width), jnp.bfloat16), pltpu.SemaphoreType.DMA((local // TILE,))]
    else:
        out_shape = (jax.ShapeDtypeStruct((local, width), jnp.float32),) * 3
        out_specs = (WHOLE,) * 3
    return pl.pallas_call(
        functools.partial(prefix_kernel, last, len(states), len(pieces)),
        out_shape=out_shape,
        in_specs=[WHOLE] * (1 + len(flat) + len(pieces)),
        out_specs=out_specs,
        scratch_shapes=scratch,
        compiler_params=PARAMS,
        cost_estimate=cost(local * (width // HD) * sum(p.shape[0] for p in pieces), 10 << 20),
        name="prefix_last" if last else "prefix",
    )(q, *flat, *pieces)


def on_device(queries, keys, values, q_gain, k_gain, positions, prefix_cache, owner):
    local = queries.shape[0]
    root = owner[0]
    root_z = (root // NC) % NZ
    q_gain, k_gain = (1.0 + q_gain)[None], (1.0 + k_gain)[None]
    first = (lax.axis_index(SEQ) == 0).astype(jnp.int32).reshape(1)

    whole = prefix_cache[0]
    half_rows = whole.shape[0] // NC
    sibling = swapped(moved(other_half_kernel, half_rows, whole), "core")
    onward = [(i, i + 1) for i in range(YH * NZ * NC - 1)]
    over_y = [(i, j) for i, j in onward if i // (NZ * NC) != j // (NZ * NC)]
    along_z = [pair for pair in onward if pair not in over_y]
    tail = jnp.concatenate([keys[local - WINDOW :], values[local - WINDOW :]], axis=1)
    sent = moved(far_quarter_kernel, half_rows // YH, whole, sibling, owner=owner)
    before = lax.ppermute(tail, SEQ, along_z)
    sent, positions = lax.optimization_barrier((sent, positions))
    came = swapped(sent, "yh")
    slab = moved(own_quarter_kernel, half_rows // YH, whole, sibling, came, owner=owner)

    half = HD // 2
    freq = 10000.0 ** (-(jnp.arange(half).astype(jnp.float32) * 2.0) / HD)
    extended = positions[0] + jnp.arange(-WINDOW, local, dtype=jnp.int32)
    angle = extended.astype(jnp.float32)[:, None] * freq[None, :]
    cosine, sine = jnp.cos(angle), jnp.sin(angle)
    query, key = normed_part(
        prep_kernel,
        PARAMS,
        (
            jax.ShapeDtypeStruct(queries.shape, jnp.bfloat16),
            jax.ShapeDtypeStruct(keys.shape, jnp.bfloat16),
        ),
        queries, keys, q_gain, k_gain, cosine, sine,
    )
    slab, query, before, tail = lax.optimization_barrier((slab, query, before, tail))
    before_over_y = lax.ppermute(tail, SEQ, over_y)

    rows, wide = slab.shape
    parts = slab.reshape(NZ, rows // NZ, NH, wide // NH).transpose(0, 2, 1, 3)
    parts = parts.reshape(NZ * NH, rows // NZ, wide // NH)
    parts = lax.all_to_all(parts, ("z", "head"), split_axis=0, concat_axis=0, tiled=True)

    upper = local_part(WINDOW, local, first, query, key, values, ALONE)
    parts, top = lax.optimization_barrier((parts, upper[0]))
    upper = (top, *upper[1:])
    mine = pick(parts.reshape(NZ, NH, rows // NZ, wide // NH), root_z)
    mine = mine.reshape(NH * rows // NZ, wide // NH)
    mine, order = lax.optimization_barrier((mine, first))

    far = swapped(mine, "yh")
    lower = local_part(0, WINDOW, order, query, key, values, PARAMS)
    far, top = lax.optimization_barrier((far, lower[0]))
    lower = (top, *lower[1:])
    pair = jnp.concatenate([mine, far], axis=0)
    pair, before = lax.optimization_barrier((pair, before))

    second = [round_z(pair, NZ // 2), round_z(pair, 2), round_z(pair, -2)]
    (key_before,) = normed_part(
        halo_kernel,
        PARAMS,
        (jax.ShapeDtypeStruct((WINDOW, keys.shape[1]), jnp.bfloat16),),
        before, before_over_y, k_gain, cosine, sine,
    )
    lower = before_part(first, query, key_before, before, before_over_y, lower)
    second, top = lax.optimization_barrier((second, lower[0]))
    lower = (top, *lower[1:])
    near = jnp.concatenate([pair, *second], axis=0)
    near_sibling = swapped(near, "core")
    double = jnp.concatenate([pair, second[0]], axis=0)
    third = [round_z(double, 1), round_z(double, -1)]
    state = prefix_part(False, query, [lower, upper], near, near_sibling)
    third, top = lax.optimization_barrier((third, state[0]))
    third = jnp.concatenate(third, axis=0)
    third_sibling = swapped(third, "core")
    state = prefix_part(False, query, [(top, *state[1:])], third)
    return prefix_part(True, query, [state], third_sibling)


def solution(mesh):
    fine = Mesh(mesh.devices.reshape(YH, NZ, NC, NH), SEQ + ("head",))
    return jax.shard_map(
        on_device,
        mesh=fine,
        in_specs=(
            P(SEQ, "head"),
            P(SEQ, "head"),
            P(SEQ, "head"),
            P(),
            P(),
            P(SEQ),
            P(SEQ, "head", None),
            P(),
        ),
        out_specs=P(SEQ, "head"),
        check_vma=False,
    )
```

```python
import functools

import jax
import jax.numpy as jnp
from jax import lax
from jax.experimental import pallas as pl
from jax.experimental.pallas import tpu as pltpu
from jax.sharding import Mesh, PartitionSpec as P

HD = 128
WINDOW = 1024
QSCALAR = 168
YH, NZ, NC, NH = 2, 8, 2, 8
SEQ = ("yh", "z", "core")
BAND_TILE = 256
TILE = 512
CHUNK = 256
NEG = -1e30
BIG = 1e30
VMEM_LIMIT = 24 * 1024 * 1024


def swapped(array, axis):
    return lax.ppermute(array, axis, [(0, 1), (1, 0)])


def round_z(array, r):
    return lax.ppermute(array, "z", [(i, (i + r) % NZ) for i in range(NZ)])


def pick(array, at):
    return lax.dynamic_index_in_dim(array, at, 0, keepdims=False)


def owner_at(owner_ref):
    root = owner_ref[0]
    return root // (NZ * NC), (root // NC) % NZ, root % NC


def copied(source, target, sems):
    rows = target.shape[0] // sems.shape[0]
    copies = [
        pltpu.make_async_copy(
            source.at[pl.ds(i * rows, rows)], target.at[pl.ds(i * rows, rows)], sems.at[i]
        )
        for i in range(sems.shape[0])
    ]
    for copy in copies:
        copy.start()
    for copy in copies:
        copy.wait()


def other_half_kernel(slab_ref, out_ref, sems):
    rows = out_ref.shape[0]
    copied(slab_ref.at[pl.ds((1 - lax.axis_index("core")) * rows, rows)], out_ref, sems)


def quarter_of(owner_ref, slab_ref, sibling_ref, of_y, out_ref, sems):
    core, rows = lax.axis_index("core"), out_ref.shape[0]
    mine = owner_at(owner_ref)[2] == core

    @pl.when(mine)
    def _():
        copied(slab_ref.at[pl.ds((core * YH + of_y) * rows, rows)], out_ref, sems)

    @pl.when(jnp.logical_not(mine))
    def _():
        out_ref[...] = sibling_ref[rows_at(of_y, rows), :]


def far_quarter_kernel(owner_ref, slab_ref, sibling_ref, out_ref, sems):
    quarter_of(owner_ref, slab_ref, sibling_ref, 1 - lax.axis_index("yh"), out_ref, sems)


def own_quarter_kernel(owner_ref, slab_ref, sibling_ref, came_ref, out_ref, sems):
    y = lax.axis_index("yh")
    mine = owner_at(owner_ref)[0] == y

    @pl.when(mine)
    def _():
        quarter_of(owner_ref, slab_ref, sibling_ref, y, out_ref, sems)

    @pl.when(jnp.logical_not(mine))
    def _():
        out_ref[...] = came_ref[...]


def moved(kernel, rows, slab, *received, owner=None):
    front = [] if owner is None else [owner]
    return pl.pallas_call(
        kernel,
        out_shape=jax.ShapeDtypeStruct((rows, slab.shape[1]), jnp.bfloat16),
        in_specs=[pl.BlockSpec(memory_space=pltpu.SMEM)] * len(front)
        + [pl.BlockSpec(memory_space=pltpu.HBM)]
        + [pl.BlockSpec(memory_space=pltpu.VMEM)] * len(received),
        out_specs=pl.BlockSpec(memory_space=pltpu.VMEM),
        scratch_shapes=[pltpu.SemaphoreType.DMA((4,))],
        compiler_params=pltpu.CompilerParams(vmem_limit_bytes=12 * 1024 * 1024),
        name="slab_rows",
    )(*front, slab, *received)


def tables(cos_ref, sin_ref, at, gain, scale):
    cosine, sine = cos_ref[at, :], sin_ref[at, :]
    cosine = jnp.concatenate([cosine, cosine], axis=1)
    sine = jnp.concatenate([-sine, sine], axis=1)
    return cosine * (gain * scale), sine * (pltpu.roll(gain, HD // 2, 1) * scale)


def normed(rows, direct, crossed):
    wide = rows.astype(jnp.float32)
    square = wide * wide
    high = square.astype(jnp.bfloat16)
    low = (square - high.astype(jnp.float32)).astype(jnp.bfloat16)
    even = jnp.full((HD, HD), 1.0 / HD, jnp.bfloat16)
    mean_sq = jnp.dot(high, even, preferred_element_type=jnp.float32)
    mean_sq = mean_sq + jnp.dot(low, even, preferred_element_type=jnp.float32)
    other = pltpu.roll(rows, HD // 2, 1).astype(jnp.float32)
    return ((wide * direct + other * crossed) * lax.rsqrt(mean_sq + 1e-06)).astype(jnp.bfloat16)


def dot_t(a, b):
    return lax.dot_general(a, b, (((1,), (1,)), ((), ())), preferred_element_type=jnp.float32)


def rows_at(t, tile):
    return pl.ds(pl.multiple_of(t * tile, tile), tile)


def columns_of(h):
    return slice(h * HD, (h + 1) * HD)


def stacked(ref, at, heads):
    return jnp.concatenate([ref[at, columns_of(h)] for h in heads], axis=0)


def prep_kernel(q_ref, k_ref, qg_ref, kg_ref, cos_ref, sin_ref, qn_ref, kn_ref):
    def own(t, _):
        at = rows_at(t, BAND_TILE)
        at_table = rows_at(t + WINDOW // BAND_TILE, BAND_TILE)
        q_tables = tables(cos_ref, sin_ref, at_table, qg_ref[...], QSCALAR ** (-0.5))
        k_tables = tables(cos_ref, sin_ref, at_table, kg_ref[...], 1.0)
        for c in range(k_ref.shape[1] // HD):
            kn_ref[at, columns_of(c)] = normed(k_ref[at, columns_of(c)], *k_tables)
        for h in range(q_ref.shape[1] // HD):
            qn_ref[at, columns_of(h)] = normed(q_ref[at, columns_of(h)], *q_tables)
        return 0

    lax.fori_loop(0, q_ref.shape[0] // BAND_TILE, own, 0)


def halo_kernel(near_ref, far_ref, kg_ref, cos_ref, sin_ref, kn_ref):
    def one(t, _):
        at = rows_at(t, BAND_TILE)
        k_tables = tables(cos_ref, sin_ref, at, kg_ref[...], 1.0)
        for c in range(kn_ref.shape[1] // HD):
            rows = near_ref[at, columns_of(c)] + far_ref[at, columns_of(c)]
            kn_ref[at, columns_of(c)] = normed(rows, *k_tables)
        return 0

    lax.fori_loop(0, WINDOW // BAND_TILE, one, 0)


def attend(state, query, key, value, keep_score=None, dead=None):
    score = dot_t(query, key)
    if keep_score is not None:
        score = jnp.where(keep_score, score, NEG)
    top = jnp.max(score, axis=1, keepdims=True)
    if dead is not None:
        top = jnp.where(dead, NEG, top)
    top = jnp.broadcast_to(top, query.shape)
    if state is not None:
        top = jnp.maximum(state[0], top)
    minus = top if dead is None else jnp.where(dead, BIG, top)
    weight = jnp.concatenate(
        [jnp.exp(score[:, i : i + HD] - minus).astype(jnp.bfloat16) for i in range(0, score.shape[1], HD)],
        axis=1,
    )
    value = jnp.concatenate([value, jnp.ones_like(value)], axis=1)
    out = jnp.dot(weight, value, preferred_element_type=jnp.float32)
    summed, total = out[:, :HD], out[:, HD:]
    if state is not None:
        keep = jnp.exp(state[0] - top)
        summed, total = state[1] * keep + summed, state[2] * keep + total
    return top, summed, total


def triangle(group):
    rows_in = lax.broadcasted_iota(jnp.int32, (group * BAND_TILE, CHUNK), 0) % BAND_TILE
    columns_in = lax.broadcasted_iota(jnp.int32, (group * BAND_TILE, CHUNK), 1)
    return columns_in <= rows_in


def kept(refs, at, kv, group, state):
    for c in range(kv):
        for g in range(group):
            rows = slice(g * BAND_TILE, (g + 1) * BAND_TILE)
            for ref, value in zip(refs, state[c]):
                ref[at, columns_of(c * group + g)] = value[rows]


def local_kernel(from_tile, order_ref, q_ref, k_ref, v_ref, *outs):
    kv = k_ref.shape[1] // HD
    group = q_ref.shape[1] // HD // kv
    reach = WINDOW // CHUNK
    late = triangle(group)
    for t in range(outs[0].shape[0] // BAND_TILE):
        at = slice(t * BAND_TILE, (t + 1) * BAND_TILE)
        block = from_tile + t
        at_query = slice(block * BAND_TILE, (block + 1) * BAND_TILE)
        state = [None] * kv
        for e in range(block, max(block - reach, 0) - 1, -1):
            keys_at = slice(e * CHUNK, (e + 1) * CHUNK)
            for c in range(kv):
                state[c] = attend(
                    state[c],
                    stacked(q_ref, at_query, range(c * group, (c + 1) * group)),
                    k_ref[keys_at, columns_of(c)],
                    v_ref[keys_at, columns_of(c)],
                    keep_score=late if e == block else ~late if e == block - reach else None,
                )
        kept(outs, at, kv, group, state)


def before_kernel(first_ref, q_ref, k_ref, near_ref, far_ref, *rest):
    ins, outs = rest[:3], rest[3:]
    kv = k_ref.shape[1] // HD
    group = q_ref.shape[1] // HD // kv
    late = triangle(group)
    is_first = first_ref[0] == 1
    for t in range(ins[0].shape[0] // BAND_TILE):
        at = slice(t * BAND_TILE, (t + 1) * BAND_TILE)
        heads = [range(c * group, (c + 1) * group) for c in range(kv)]
        state = [tuple(stacked(ref, at, heads[c]) for ref in ins) for c in range(kv)]
        for e in range(WINDOW // CHUNK - 1, t - 1, -1):
            keys_at = slice(e * CHUNK, (e + 1) * CHUNK)
            for c in range(kv):
                state[c] = attend(
                    state[c],
                    stacked(q_ref, at, heads[c]),
                    k_ref[keys_at, columns_of(c)],
                    near_ref[keys_at, columns_of(kv + c)] + far_ref[keys_at, columns_of(kv + c)],
                    keep_score=~late if e == t else None,
                    dead=is_first,
                )
        kept(outs, at, kv, group, state)


def blocks_of(p_refs):
    blocks, held, room = [], [], CHUNK
    for p_ref in p_refs:
        start = 0
        while start < p_ref.shape[0]:
            rows = min(room, p_ref.shape[0] - start)
            held.append((p_ref, start, rows))
            start, room = start + rows, room - rows
            if room == 0:
                blocks.append(held)
                held, room = [], CHUNK
    if held and blocks and CHUNK - room < CHUNK:
        blocks[-1] = blocks[-1] + held
    elif held:
        blocks.append(held)
    return blocks


def joined(block, h):
    parts = [p_ref[start : start + rows, columns_of(h)] for p_ref, start, rows in block]
    return parts[0] if len(parts) == 1 else jnp.concatenate(parts, axis=0)


def prefix_kernel(last, bands, pieces, q_ref, *rest):
    states, rest = [rest[3 * i : 3 * i + 3] for i in range(bands)], rest[3 * bands :]
    p_refs, outs = rest[:pieces], rest[pieces:]
    if last:
        out_ref, store_ref, sems = outs
        outs = (store_ref,)
        sent = [
            pltpu.make_async_copy(store_ref.at[rows_at(t, TILE)], out_ref.at[rows_at(t, TILE)], sems.at[t])
            for t in range(q_ref.shape[0] // TILE)
        ]
    kv = p_refs[0].shape[1] // (2 * HD)
    group = q_ref.shape[1] // HD // kv
    state_of = [(refs, at) for refs in states for at in range(0, refs[0].shape[0], TILE)]

    def step(t, state_refs, at_in):
        at = rows_at(t, TILE)
        heads = [range(c * group, (c + 1) * group) for c in range(kv)]
        queries = [stacked(q_ref, at, heads[c]) for c in range(kv)]
        state = [tuple(stacked(ref, at_in, heads[c]) for ref in state_refs) for c in range(kv)]
        for block in blocks_of(p_refs):
            for c in range(kv):
                state[c] = attend(state[c], queries[c], joined(block, 2 * c), joined(block, 2 * c + 1))
        for c in range(kv):
            result = [(state[c][1] / state[c][2]).astype(jnp.bfloat16)] if last else state[c]
            for g in range(group):
                rows = slice(g * TILE, (g + 1) * TILE)
                for ref, part in zip(outs, result):
                    ref[at, columns_of(c * group + g)] = part[rows]

    if bands > 1:
        for i in range(q_ref.shape[0] // TILE):
            refs, start = state_of[i]
            step(i, refs, slice(start, start + TILE))
    elif last:
        for t in range(q_ref.shape[0] // TILE):
            step(t, states[0], slice(t * TILE, (t + 1) * TILE))
            sent[t].start()
        for copy in sent:
            copy.wait()
    else:

        def one(t, _):
            step(t, states[0], rows_at(t, TILE))
            return 0

        lax.fori_loop(0, q_ref.shape[0] // TILE, one, 0)


WHOLE = pl.BlockSpec(memory_space=pltpu.VMEM)
ALONE = pltpu.CompilerParams(vmem_limit_bytes=60 * 1024 * 1024)
IN_HBM = pl.BlockSpec(memory_space=pltpu.HBM)
PARAMS = pltpu.CompilerParams(vmem_limit_bytes=VMEM_LIMIT)


def cost(pairs, in_out):
    return pl.CostEstimate(flops=8 * pairs * HD, transcendentals=pairs, bytes_accessed=in_out)


def normed_part(kernel, params, outs, *args):
    size = sum(o.size for o in outs)
    return pl.pallas_call(
        kernel,
        out_shape=outs,
        in_specs=[WHOLE] * len(args),
        out_specs=(WHOLE,) * len(outs),
        compiler_params=params,
        cost_estimate=pl.CostEstimate(flops=size, transcendentals=0, bytes_accessed=size),
        name="norm_rope",
    )(*args)


def local_part(from_row, to_row, order, q, k, v, params):
    width, wide = q.shape[1], k.shape[1]
    rows = to_row - from_row
    return pl.pallas_call(
        functools.partial(local_kernel, from_row // BAND_TILE),
        out_shape=(jax.ShapeDtypeStruct((rows, width), jnp.float32),) * 3,
        in_specs=[pl.BlockSpec(memory_space=pltpu.SMEM)] + [WHOLE] * 3,
        out_specs=(WHOLE,) * 3,
        compiler_params=params,
        cost_estimate=cost(rows * (width // HD) * WINDOW, 5 << 20),
        name="band_local",
    )(order, q, k, v)


def before_part(first, q, key_before, near, far, state):
    width, wide = q.shape[1], key_before.shape[1]
    rows = state[0].shape[0]
    return pl.pallas_call(
        before_kernel,
        out_shape=(jax.ShapeDtypeStruct((rows, width), jnp.float32),) * 3,
        in_specs=[pl.BlockSpec(memory_space=pltpu.SMEM)] + [WHOLE] * 7,
        out_specs=(WHOLE,) * 3,
        compiler_params=PARAMS,
        cost_estimate=cost(rows * (width // HD) * WINDOW // 2, 5 << 20),
        name="band_before",
    )(first, q, key_before, near, far, *state)


def prefix_part(last, q, states, *pieces):
    local, width = q.shape
    flat = [part for state in states for part in state]
    scratch = []
    if last:
        out_shape = jax.ShapeDtypeStruct((local, width), jnp.bfloat16)
        out_specs = IN_HBM
        scratch = [pltpu.VMEM((local, width), jnp.bfloat16), pltpu.SemaphoreType.DMA((local // TILE,))]
    else:
        out_shape = (jax.ShapeDtypeStruct((local, width), jnp.float32),) * 3
        out_specs = (WHOLE,) * 3
    return pl.pallas_call(
        functools.partial(prefix_kernel, last, len(states), len(pieces)),
        out_shape=out_shape,
        in_specs=[WHOLE] * (1 + len(flat) + len(pieces)),
        out_specs=out_specs,
        scratch_shapes=scratch,
        compiler_params=PARAMS,
        cost_estimate=cost(local * (width // HD) * sum(p.shape[0] for p in pieces), 10 << 20),
        name="prefix_last" if last else "prefix",
    )(q, *flat, *pieces)


def on_device(queries, keys, values, q_gain, k_gain, positions, prefix_cache, owner):
    local = queries.shape[0]
    root = owner[0]
    root_z = (root // NC) % NZ
    q_gain, k_gain = (1.0 + q_gain)[None], (1.0 + k_gain)[None]
    first = (lax.axis_index(SEQ) == 0).astype(jnp.int32).reshape(1)

    whole = prefix_cache[0]
    half_rows = whole.shape[0] // NC
    sibling = swapped(moved(other_half_kernel, half_rows, whole), "core")
    onward = [(i, i + 1) for i in range(YH * NZ * NC - 1)]
    over_y = [(i, j) for i, j in onward if i // (NZ * NC) != j // (NZ * NC)]
    along_z = [pair for pair in onward if pair not in over_y]
    tail = jnp.concatenate([keys[local - WINDOW :], values[local - WINDOW :]], axis=1)
    sent = moved(far_quarter_kernel, half_rows // YH, whole, sibling, owner=owner)
    before = lax.ppermute(tail, SEQ, along_z)
    sent, positions = lax.optimization_barrier((sent, positions))
    came = swapped(sent, "yh")
    slab = moved(own_quarter_kernel, half_rows // YH, whole, sibling, came, owner=owner)

    half = HD // 2
    freq = 10000.0 ** (-(jnp.arange(half).astype(jnp.float32) * 2.0) / HD)
    extended = positions[0] + jnp.arange(-WINDOW, local, dtype=jnp.int32)
    angle = extended.astype(jnp.float32)[:, None] * freq[None, :]
    cosine, sine = jnp.cos(angle), jnp.sin(angle)
    query, key = normed_part(
        prep_kernel,
        PARAMS,
        (
            jax.ShapeDtypeStruct(queries.shape, jnp.bfloat16),
            jax.ShapeDtypeStruct(keys.shape, jnp.bfloat16),
        ),
        queries, keys, q_gain, k_gain, cosine, sine,
    )
    slab, query, before, tail = lax.optimization_barrier((slab, query, before, tail))
    before_over_y = lax.ppermute(tail, SEQ, over_y)

    rows, wide = slab.shape
    parts = slab.reshape(NZ, rows // NZ, NH, wide // NH).transpose(0, 2, 1, 3)
    parts = parts.reshape(NZ * NH, rows // NZ, wide // NH)
    parts = lax.all_to_all(parts, ("z", "head"), split_axis=0, concat_axis=0, tiled=True)

    upper = local_part(WINDOW, local, first, query, key, values, ALONE)
    parts, top = lax.optimization_barrier((parts, upper[0]))
    upper = (top, *upper[1:])
    mine = pick(parts.reshape(NZ, NH, rows // NZ, wide // NH), root_z)
    mine = mine.reshape(NH * rows // NZ, wide // NH)
    mine, order = lax.optimization_barrier((mine, first))

    far = swapped(mine, "yh")
    lower = local_part(0, WINDOW, order, query, key, values, PARAMS)
    far, top = lax.optimization_barrier((far, lower[0]))
    lower = (top, *lower[1:])
    pair = jnp.concatenate([mine, far], axis=0)
    pair, before = lax.optimization_barrier((pair, before))

    second = [round_z(pair, NZ // 2), round_z(pair, 2), round_z(pair, -2)]
    (key_before,) = normed_part(
        halo_kernel,
        PARAMS,
        (jax.ShapeDtypeStruct((WINDOW, keys.shape[1]), jnp.bfloat16),),
        before, before_over_y, k_gain, cosine, sine,
    )
    lower = before_part(first, query, key_before, before, before_over_y, lower)
    second, top = lax.optimization_barrier((second, lower[0]))
    lower = (top, *lower[1:])
    near = jnp.concatenate([pair, *second], axis=0)
    near_sibling = swapped(near, "core")
    double = jnp.concatenate([pair, second[0]], axis=0)
    third = [round_z(double, 1), round_z(double, -1)]
    state = prefix_part(False, query, [lower, upper], near, near_sibling)
    third, top = lax.optimization_barrier((third, state[0]))
    third = jnp.concatenate(third, axis=0)
    third_sibling = swapped(third, "core")
    state = prefix_part(False, query, [(top, *state[1:])], third)
    return prefix_part(True, query, [state], third_sibling)


def solution(mesh):
    fine = Mesh(mesh.devices.reshape(YH, NZ, NC, NH), SEQ + ("head",))
    return jax.shard_map(
        on_device,
        mesh=fine,
        in_specs=(
            P(SEQ, "head"),
            P(SEQ, "head"),
            P(SEQ, "head"),
            P(),
            P(),
            P(SEQ),
            P(SEQ, "head", None),
            P(),
        ),
        out_specs=P(SEQ, "head"),
        check_vma=False,
    )
```
